32 devices in a mesh: parts: 2 (over y), seq: 4 (over z), head: 4 (over x, core).
Axes of the slice: x: 2, y: 2, z: 4, core: 2. Of those that a mesh axis runs over, the one named last changes fastest.
Arguments:
- query_rows: bfloat16 [6144, 4096], P(('parts', 'seq', 'head')), parts along dimension 0, may hold values from -12 to 12
- key_rows: bfloat16 [6144, 4096], P(('parts', 'seq', 'head')), parts along dimension 0, may hold values from -12 to 12
- value_rows: bfloat16 [6144, 4096], P(('parts', 'seq', 'head')), parts along dimension 0, may hold values from -6 to 6
- block_lists: int32 [64, 4, 4, 3], P('parts', 'seq'), parts along dimension 0, may hold values from 0 to 5, as said below
- block_counts: int32 [64, 4, 4], P('parts'), parts along dimension 0, may hold values from 0 to 3, as said below
Outputs:
- attended: bfloat16 [6144, 4096], P(('parts', 'seq', 'head')), parts along dimension 0
The draws below stay inside these ranges and needn't reach their ends.
There are 2 independent parts, one for each index of `parts`. The reference program is written for one: setup_inputs(seed, part) draws one part's arguments, and reference() takes and returns one part's arrays. A program takes and returns all parts, laid end to end along the dimension named above; each array names one. Nothing has to cross between parts.
Inputs may be any that keep to these rules, and one draw needn't show every extreme that they name: `block_lists`: for one head, query tile and key tile the 3 entries are distinct block numbers of the key tile; only the first block_counts of them are listed. `block_counts`: 0 where the key tile is the query tile; some entries of every draw equal 3; for every k, query tile and key tile, the counts of heads 2k and 2k+1 sum to at most 4, and exactly 4 for some k in every draw.
All inputs are finite; a program needn't handle non-finite values.
Results may differ from the reference program's by a relative error of at most 0.0034.
Values may be sent and summed in bfloat16 or wider, within the bound.
A program may use at most 64 MiB of HBM per device.

```python
import math
import jax
import jax.numpy as jnp
from jax import lax

HEADS = 32
DH = 128
BLOCK = 128
MOST = 3
PAIR_MOST = 4
TILE = 768
TILES = 4
SEQ_LEN = 3072


def draw_query_rows(key, part):
    bulk = jnp.clip(1.75 * jax.random.normal(jax.random.fold_in(key, 41), (SEQ_LEN, HEADS * DH), jnp.float32), -12.0, 12.0)
    return bulk.astype(jnp.bfloat16)


def draw_key_rows(key, part):
    bulk = jnp.clip(1.75 * jax.random.normal(jax.random.fold_in(key, 43), (SEQ_LEN, HEADS * DH), jnp.float32), -12.0, 12.0)
    return bulk.astype(jnp.bfloat16)


def draw_block_lists(key, part):
    block_total = TILE // BLOCK
    scores = jax.random.randint(jax.random.fold_in(key, 21), (HEADS, TILES, TILES, block_total), 0, 1 << 20)
    scores = scores * block_total + jnp.arange(block_total, dtype=jnp.int32)
    return lax.top_k(scores, MOST)[1].astype(jnp.int32)


def draw_block_counts(key, part):
    pair_total = HEADS // 2
    density_level = jax.random.permutation(jax.random.fold_in(key, 31), pair_total) % 3
    busy_sum = jax.random.randint(jax.random.fold_in(key, 32), (pair_total, TILES, TILES), MOST, PAIR_MOST + 1)
    sparse_sum = jax.random.randint(jax.random.fold_in(key, 33), (pair_total, TILES, TILES), 0, 2)
    level_grid = density_level[:, None, None]
    pair_sum = jnp.where(level_grid == 2, PAIR_MOST, jnp.where(level_grid == 1, busy_sum, sparse_sum))
    lower_end = jnp.maximum(pair_sum - MOST, 0)
    upper_end = jnp.minimum(pair_sum, MOST)
    split_draw = jax.random.randint(jax.random.fold_in(key, 34), (pair_total, TILES, TILES), 0, 1 << 20)
    first_count = lower_end + split_draw % (upper_end - lower_end + 1)
    first_count = jnp.where(level_grid == 2, MOST, first_count)
    second_count = pair_sum - first_count
    counts_grid = jnp.stack([first_count, second_count], axis=1).reshape(HEADS, TILES, TILES)
    own_tile = jnp.arange(TILES)[:, None] == jnp.arange(TILES)[None, :]
    return jnp.where(own_tile[None], 0, counts_grid).astype(jnp.int32)


def steps_of(key, dims, split, least, high):
    level, own = 1.0, jax.random.fold_in(key, 6)
    for position, blocks in split:
        heights = jnp.exp(jax.random.uniform(jax.random.fold_in(own, position), (blocks,), jnp.float32, least / len(split), high / len(split)))
        level = level * jnp.repeat(heights, dims[position] // blocks).reshape([-1 if axis == position else 1 for axis in range(len(dims))])
    return level


def centred(stream_key, extent, deviation, bound, split=(), held_as=jnp.bfloat16):
    factor_of = steps_of(stream_key, extent, split, -0.22, 0.18) if split else 1.0
    values = jax.random.normal(stream_key, extent, jnp.float32) * deviation * factor_of
    return jnp.minimum(jnp.maximum(values, -bound), bound).astype(held_as)


def setup_inputs(seed: int = 0, part: int = 0) -> dict:
    seeds = jax.random.split(jax.random.key(seed), 6)
    part_splits = jax.random.split(jax.random.fold_in(seeds[5], part), 6)
    query_rows = draw_query_rows(jax.random.fold_in(jax.random.fold_in(seeds[5], part), 71), part)
    key_rows = draw_key_rows(jax.random.fold_in(jax.random.fold_in(seeds[5], part), 71), part)
    value_rows = centred(part_splits[2], (SEQ_LEN, HEADS * DH), 1.0, 6.0, ((0, 16),))
    block_lists = draw_block_lists(jax.random.fold_in(jax.random.fold_in(seeds[5], part), 71), part)
    block_counts = draw_block_counts(jax.random.fold_in(jax.random.fold_in(seeds[5], part), 71), part)
    return dict(query_rows=query_rows, key_rows=key_rows, value_rows=value_rows, block_lists=block_lists, block_counts=block_counts)


def reference(query_rows, key_rows, value_rows, block_lists, block_counts):
    block_total = TILE // BLOCK
    score_scale = 1.0 / math.sqrt(DH)

    def one_head(head_index):
        head_queries = lax.dynamic_slice_in_dim(query_rows, head_index * DH, DH, 1)
        head_keys = lax.dynamic_slice_in_dim(key_rows, head_index * DH, DH, 1)
        head_values = lax.dynamic_slice_in_dim(value_rows, head_index * DH, DH, 1)
        key_blocks = head_keys.reshape(TILES * block_total, BLOCK, DH)
        value_blocks = head_values.reshape(TILES * block_total, BLOCK, DH)

        def one_tile(tile_index):
            tile_queries = lax.dynamic_slice_in_dim(head_queries, tile_index * TILE, TILE, 0)
            own_keys = lax.dynamic_slice_in_dim(head_keys, tile_index * TILE, TILE, 0)
            own_values = lax.dynamic_slice_in_dim(head_values, tile_index * TILE, TILE, 0)
            tile_lists = block_lists[head_index, tile_index].astype(jnp.int32)
            tile_counts = block_counts[head_index, tile_index].astype(jnp.int32)
            picks = (jnp.arange(TILES, dtype=jnp.int32)[:, None] * block_total + tile_lists).reshape(-1)
            live_slots = (jnp.arange(MOST, dtype=jnp.int32)[None, :] < tile_counts[:, None]).reshape(-1)
            far_keys = key_blocks[picks].reshape(TILES * MOST * BLOCK, DH)
            far_values = value_blocks[picks].reshape(TILES * MOST * BLOCK, DH)
            all_keys = jnp.concatenate([own_keys, far_keys], axis=0)
            all_values = jnp.concatenate([own_values, far_values], axis=0)
            live_keys = jnp.concatenate([jnp.ones((TILE,), bool), jnp.repeat(live_slots, BLOCK)])
            scores = jnp.dot(tile_queries, all_keys.T, preferred_element_type=jnp.float32) * score_scale
            scores = jnp.where(live_keys[None, :], scores, -jnp.inf)
            row_top = lax.optimization_barrier(jnp.max(scores, axis=1, keepdims=True))
            weights = jnp.exp(scores - row_top)
            denominator = lax.optimization_barrier(jnp.sum(weights, axis=1, keepdims=True))
            mixture = jnp.dot(weights.astype(jnp.bfloat16), all_values, preferred_element_type=jnp.float32)
            return (mixture / denominator).astype(jnp.bfloat16)
        return lax.map(one_tile, jnp.arange(TILES, dtype=jnp.int32))
    head_outputs = lax.map(one_head, jnp.arange(HEADS, dtype=jnp.int32))
    head_outputs = head_outputs.reshape(HEADS, TILES * TILE, DH)
    return jnp.transpose(head_outputs, (1, 0, 2)).reshape(TILES * TILE, HEADS * DH)
```

```python
import functools
import math

import jax
import jax.numpy as jnp
from jax import lax
from jax.experimental import pallas as pl
from jax.experimental.pallas import tpu as pltpu
from jax.sharding import PartitionSpec as P

HEADS = 32
DH = 128
BLOCK = 128
MOST = 3
PAIR_MOST = 4
TILE = 768
MESH = pl.DeviceIdType.MESH


def contract_last(a, b):
    return lax.dot_general(a, b, (((1,), (1,)), ((), ())), preferred_element_type=jnp.float32)


def slot_ranges(p, c, pairs):
    if c == 1 and p == pairs - 1:
        return [(0, MOST), (MOST, PAIR_MOST)]
    if p == 0:
        return [(0, 1), (1, PAIR_MOST)]
    return [(0, PAIR_MOST)]


def body(dims, lists_ref, counts_ref, q_ref, k_ref, v_ref, out_ref, *scratch):
    H, S, rows, heads, piece = dims
    pairs = heads // 2
    last = pairs - 1
    chips = H // 2
    kb, vb, qb = scratch[: 2 * pairs], scratch[2 * pairs : 4 * pairs], scratch[4 * pairs : 5 * pairs]
    (ob, pk, fk, pbuf, mbuf, tbuf, lbuf, lsm, csm, x_send, x_recv, z_send, z_recv, l_send, l_recv, l_loc, o_send, o_recv) = (
        scratch[5 * pairs :]
    )
    me = lax.axis_index("head")
    tile = lax.axis_index("seq")

    def peer_of(i):
        chip = lax.rem(lax.div(me, 2) + 1 + lax.div(i, 2), chips)
        return chip * 2 + lax.rem(me + i + 1, 2)

    def source_of(i):
        chip = lax.rem(lax.div(me, 2) + 2 * chips - 1 - lax.div(i, 2), chips)
        return chip * 2 + lax.rem(me + i + 1, 2)

    def tile_after(d):
        return lax.rem(tile + d, S)

    def i32(i):
        return jnp.int32(i)

    counts_copy = pltpu.make_async_copy(counts_ref, csm, l_loc.at[0])
    counts_copy.start()
    barrier = pltpu.get_barrier_semaphore()
    for d in range(1, S):
        pl.semaphore_signal(barrier, inc=1, device_id={"seq": tile_after(d)}, device_id_type=MESH)
    for i in range(H - 1):
        pl.semaphore_signal(barrier, inc=1, device_id={"head": peer_of(i32(i))}, device_id_type=MESH)

    sources = (k_ref, v_ref, q_ref)

    def head_columns(owner, p, hs):
        return pl.ds(pl.multiple_of((owner * heads + 2 * p + hs) * DH, DH), DH)

    def pair_columns(owner, p):
        return pl.ds(pl.multiple_of((owner * heads + 2 * p) * DH, 2 * DH), 2 * DH)

    def row_range(owner):
        return pl.ds(pl.multiple_of(owner * rows, 16), rows)

    def source_at(a, owner, p, hs):
        if a == 2:
            return q_ref.at[:, pair_columns(owner, p)]
        return sources[a].at[:, :, head_columns(owner, p, hs)]

    def place_at(a, owner, p, hs):
        if a == 2:
            return qb[p].at[row_range(owner), :]
        held = (kb, vb)[a][2 * p + hs]
        return held.at[pl.ds(owner * (rows // piece), rows // piece)]

    def own_copy(a, p, hs):
        return pltpu.make_async_copy(source_at(a, me, p, hs), place_at(a, me, p, hs), x_recv.at[a, p, hs, H - 1])

    def x_copy(a, p, hs, i, landed):
        to = peer_of(i32(i))
        at = source_of(i32(i)) if landed else me
        return pltpu.make_async_remote_copy(
            src_ref=source_at(a, to, p, hs),
            dst_ref=place_at(a, at, p, hs),
            send_sem=x_send.at[a, p, hs, i],
            recv_sem=x_recv.at[a, p, hs, i],
            device_id={"head": to},
            device_id_type=MESH,
        )

    def l_copy(d):
        return pltpu.make_async_remote_copy(
            src_ref=lists_ref,
            dst_ref=lbuf.at[d - 1],
            send_sem=l_send.at[d - 1],
            recv_sem=l_recv.at[d - 1],
            device_id={"seq": tile_after(d)},
            device_id_type=MESH,
        )

    def z_copy(p, d, c, g):
        lo, hi = slot_ranges(p, c, pairs)[g]
        return pltpu.make_async_remote_copy(
            src_ref=pk.at[p, d - 1, c, lo:hi],
            dst_ref=fk.at[p, d - 1, c, lo:hi],
            send_sem=z_send.at[p, d - 1, c, g],
            recv_sem=z_recv.at[p, d - 1, c, g],
            device_id={"seq": tile_after(d)},
            device_id_type=MESH,
        )

    def o_copy(p, hs, i, landed):
        to = peer_of(i)
        at = source_of(i) if landed else me
        return pltpu.make_async_remote_copy(
            src_ref=ob.at[p, hs, i],
            dst_ref=out_ref.at[:, head_columns(at, p, hs)],
            send_sem=o_send.at[p, hs, i],
            recv_sem=o_recv.at[p, hs, i],
            device_id={"head": to},
            device_id_type=MESH,
        )

    def o_own(p, hs):
        return pltpu.make_async_copy(
            ob.at[p, hs, H - 1], out_ref.at[:, head_columns(me, p, hs)], o_recv.at[p, hs, H - 1]
        )

    def x_start(a, p):
        for hs in range(1 if a == 2 else 2):
            for i in range(H - 1):
                x_copy(a, p, hs, i, False).start()
            own_copy(a, p, hs).start()

    def x_arrived(a, p, hs):
        own_copy(a, p, hs).wait()
        for i in range(H - 1):
            x_copy(a, p, hs, i, True).wait_recv()

    pl.semaphore_wait(barrier, H - 1 + S - 1)
    order = []
    for p in range(pairs):
        order += [(0, p), (1, p)]
        if p >= 1:
            order.append((2, p - 1))
    order.append((2, last))
    early = order[:4]
    x_start(*early[0])
    for d in range(1, S):
        l_copy(d).start()
    for a, p in early[1:]:
        x_start(a, p)

    counts_copy.wait()
    for d in range(1, S):
        l_copy(d).wait_recv()
    to_scalars = pltpu.make_async_copy(lbuf, lsm, l_loc.at[1])
    to_scalars.start()
    to_scalars.wait()

    waited = set()

    def need(a, p, hs):
        if (a, p, hs) not in waited:
            waited.add((a, p, hs))
            x_arrived(a, p, hs)

    def pack(p, c, g):
        held = (kb, vb)[c][2 * p : 2 * p + 2]
        lo, hi = slot_ranges(p, c, pairs)[g]
        if lo < MOST:
            need(c, p, 0)
        if hi > 1:
            need(c, p, 1)
        head = me * heads + 2 * p
        for d in range(1, S):
            at = S - d - 1
            first = csm[tile_after(d), tile, head]
            for s in range(lo, hi):
                left = lsm[at, min(s, MOST - 1), tile, head]
                right = lsm[at, min(PAIR_MOST - 1 - s, MOST - 1), tile, head + 1]
                for b in range(BLOCK // piece):
                    if s < MOST:
                        chosen = held[0][left * (BLOCK // piece) + b]
                    if s > 0:
                        other = held[1][right * (BLOCK // piece) + b]
                        chosen = jnp.where(s < first, chosen, other) if s < MOST else other
                    pk[p, d - 1, c, s, pl.ds(b * piece, piece), :] = chosen
            z_copy(p, d, c, g).start()

    for p in range(pairs):
        for c in range(2):
            for g in range(len(slot_ranges(p, c, pairs))):
                pack(p, c, g)
        if p == 0:
            for a, pp in order[4:]:
                x_start(a, pp)

    factor = math.log2(math.e) / math.sqrt(DH)
    width = MOST * BLOCK
    lane = lax.broadcasted_iota(jnp.int32, (1, width), 1)

    def z_arrived(p, c, g):
        for d in range(1, S):
            z_copy(p, d, c, g).wait_recv()

    def scores_of(p, hs, q):
        scores = [contract_last(q, kb[2 * p + hs][...].reshape(TILE, DH))]
        for d in range(1, S):
            used = csm[tile, lax.rem(tile + S - d, S), me * heads + 2 * p + hs] * BLOCK
            live = lane < used if hs == 0 else lane >= width - used
            bias = jnp.where(live, 0.0, -jnp.inf).astype(jnp.float32)
            far = fk[p, d - 1, 0, hs : hs + MOST].reshape(width, DH)
            scores.append(contract_last(q, far) + bias)
        top = functools.reduce(jnp.maximum, [jnp.max(s, axis=1, keepdims=True) for s in scores])
        return scores, top

    def weigh(s, top):
        return jnp.exp2((s - top) * factor)

    def mix(w, v):
        return jnp.dot(w, v, preferred_element_type=jnp.float32)

    for p in range(last):
        need(2, p, 0)
        for c in range(2):
            for g in range(len(slot_ranges(p, c, pairs))):
                z_arrived(p, c, g)

        def chunk(i, carry, p=p):
            mine = row_range(peer_of(i))
            for hs in range(2):
                q = qb[p][mine, hs * DH : (hs + 1) * DH]
                scores, top = scores_of(p, hs, q)
                values = [vb[2 * p + hs][...].reshape(TILE, DH)]
                values += [fk[p, d - 1, 1, hs : hs + MOST].reshape(width, DH) for d in range(1, S)]
                total = jnp.zeros((rows, 1), jnp.float32)
                mixed = jnp.zeros((rows, DH), jnp.float32)
                for s, v in zip(scores, values):
                    w = weigh(s, top)
                    total = total + jnp.sum(w, axis=1, keepdims=True)
                    mixed = mixed + mix(w.astype(jnp.bfloat16), v)
                ob[p, hs, i] = (mixed / total).astype(jnp.bfloat16)

                @pl.when(i < H - 1)
                def _(hs=hs):
                    o_copy(p, hs, i, False).start()

            return carry

        lax.fori_loop(0, H, chunk, 0)
        for hs in range(2):
            o_own(p, hs).start()

    need(2, last, 0)
    for g in range(len(slot_ranges(last, 0, pairs))):
        z_arrived(last, 0, g)

    def weights_chunk(i, carry):
        mine = row_range(peer_of(i))
        for hs in range(2):
            q = qb[last][mine, hs * DH : (hs + 1) * DH]
            scores, top = scores_of(last, hs, q)
            w = weigh(scores[0], top)
            total = jnp.sum(w, axis=1, keepdims=True)
            mbuf[hs, i] = mix(w.astype(jnp.bfloat16), vb[2 * last + hs][...].reshape(TILE, DH))
            for d in range(1, S):
                w = weigh(scores[d], top)
                total = total + jnp.sum(w, axis=1, keepdims=True)
                pbuf[hs, i, :, (d - 1) * width : d * width] = w.astype(jnp.bfloat16)
            tbuf[hs, i] = total
        return carry

    lax.fori_loop(0, H, weights_chunk, 0)
    for hs in range(2):
        z_arrived(last, 1, hs)

        def values_chunk(i, carry, hs=hs):
            mixed = mbuf[hs, i]
            for d in range(1, S):
                v = fk[last, d - 1, 1, hs : hs + MOST].reshape(width, DH)
                mixed = mixed + mix(pbuf[hs, i, :, (d - 1) * width : d * width], v)
            ob[last, hs, i] = (mixed / tbuf[hs, i]).astype(jnp.bfloat16)

            @pl.when(i < H - 1)
            def _():
                o_copy(last, hs, i, False).start()

            return carry

        lax.fori_loop(0, H, values_chunk, 0)
        o_own(last, hs).start()

    for p in range(pairs):
        for hs in range(2):
            o_own(p, hs).wait()
            for i in range(H - 1):
                o_copy(p, hs, i32(i), True).wait_recv()
    for d in range(1, S):
        l_copy(d).wait_send()
        for p in range(pairs):
            for c in range(2):
                for g in range(len(slot_ranges(p, c, pairs))):
                    z_copy(p, d, c, g).wait_send()
    for p in range(pairs):
        for i in range(H - 1):
            for a in range(3):
                for hs in range(1 if a == 2 else 2):
                    x_copy(a, p, hs, i, False).wait_send()
            for hs in range(2):
                o_copy(p, hs, i32(i), False).wait_send()


def on_device(query_rows, key_rows, value_rows, block_lists, block_counts):
    H = lax.axis_size("head")
    S = lax.axis_size("seq")
    rows = query_rows.shape[0]
    heads = HEADS // H
    pairs = heads // 2
    lists = jnp.transpose(block_lists, (1, 3, 2, 0))[0]
    counts = jnp.transpose(block_counts, (1, 2, 0))
    bf16 = jnp.bfloat16
    piece = math.gcd(rows, BLOCK)
    pieces = (rows // piece, piece, query_rows.shape[1])
    hbm = pl.BlockSpec(memory_space=pltpu.HBM)
    return pl.pallas_call(
        functools.partial(body, (H, S, rows, heads, piece)),
        out_shape=pltpu.VMEM(query_rows.shape, bf16),
        in_specs=[hbm] * 5,
        out_specs=pl.BlockSpec(memory_space=pl.ANY),
        scratch_shapes=[pltpu.VMEM((TILE // piece, piece, DH), bf16) for _ in range(4 * pairs)]
        + [pltpu.VMEM((TILE, 2 * DH), bf16) for _ in range(pairs)]
        + [
            pltpu.VMEM((pairs, 2, H, rows, DH), bf16),
            pltpu.VMEM((pairs, S - 1, 2, PAIR_MOST, BLOCK, DH), bf16),
            pltpu.VMEM((pairs, S - 1, 2, PAIR_MOST, BLOCK, DH), bf16),
            pltpu.VMEM((2, H, rows, (S - 1) * MOST * BLOCK), bf16),
            pltpu.VMEM((2, H, rows, DH), jnp.float32),
            pltpu.VMEM((2, H, rows, 1), jnp.float32),
            pltpu.VMEM((S - 1,) + lists.shape, jnp.int32),
            pltpu.SMEM((S - 1,) + lists.shape, jnp.int32),
            pltpu.SMEM(counts.shape, jnp.int32),
            pltpu.SemaphoreType.DMA((3, pairs, 2, H)),
            pltpu.SemaphoreType.DMA((3, pairs, 2, H)),
            pltpu.SemaphoreType.DMA((pairs, S - 1, 2, 2)),
            pltpu.SemaphoreType.DMA((pairs, S - 1, 2, 2)),
            pltpu.SemaphoreType.DMA((S - 1,)),
            pltpu.SemaphoreType.DMA((S - 1,)),
            pltpu.SemaphoreType.DMA((2,)),
            pltpu.SemaphoreType.DMA((pairs, 2, H)),
            pltpu.SemaphoreType.DMA((pairs, 2, H)),
        ],
        compiler_params=pltpu.CompilerParams(
            collective_id=0, has_side_effects=True, vmem_limit_bytes=60 << 20
        ),
        name="block_attention",
    )(lists, counts, query_rows, key_rows.reshape(pieces), value_rows.reshape(pieces))


def solution(mesh):
    in_specs = (
        P(("parts", "seq", "head"), None),
        P(("parts", "seq", "head"), None),
        P(("parts", "seq", "head"), None),
        P("parts", "seq", None, None),
        P("parts", None, None),
    )
    out_specs = P(("parts", "seq", "head"), None)
    return jax.shard_map(
        on_device, mesh=mesh, in_specs=in_specs, out_specs=out_specs, check_vma=False
    )
```

```python
import functools
import math

import jax
import jax.numpy as jnp
from jax import lax
from jax.experimental import pallas as pl
from jax.experimental.pallas import tpu as pltpu
from jax.sharding import PartitionSpec as P

HEADS = 32
DH = 128
BLOCK = 128
MOST = 3
PAIR_MOST = 4
TILE = 768
MESH = pl.DeviceIdType.MESH
ROOMS = (1, PAIR_MOST)
VMEM_LIMIT = 60 << 20


def contract_last(a, b):
    return lax.dot_general(a, b, (((1,), (1,)), ((), ())), preferred_element_type=jnp.float32)


def rank_at(H, pairs, h, p):
    if pairs != 4:
        return p * H + h
    chips = H // 2
    if p == 2:
        return 2 * H + lax.rem(h, 2) * chips + lax.div(h, 2)
    return {0: 0, 1: 3 * H, 3: H}[p] + h


def heavy_pairs(H, pairs):
    return 2 * H + H // 2 if pairs == 4 else H * pairs


def ranked(counts, H, pairs):
    total = HEADS // 2
    f32 = jnp.float32
    head_no = lax.broadcasted_iota(jnp.int32, (HEADS, total), 0)
    pair_no = lax.broadcasted_iota(jnp.int32, (HEADS, total), 1)
    in_pair = jnp.where((head_no == 2 * pair_no) | (head_no == 2 * pair_no + 1), 1.0, 0.0).astype(f32)
    most = jnp.zeros((1, total), f32)
    for t in range(counts.shape[0]):
        sums = jnp.dot(counts[t].astype(f32), in_pair, preferred_element_type=f32)
        most = jnp.maximum(most, jnp.max(sums, axis=0, keepdims=True))
    row = lax.broadcasted_iota(jnp.int32, (total, total), 0)
    col = lax.broadcasted_iota(jnp.int32, (total, total), 1)
    along = jnp.broadcast_to(most, (total, total))
    down = jnp.sum(jnp.where(row == col, along, 0.0), axis=1, keepdims=True)
    ahead = (along > down) | ((along == down) & (col < row))
    rank = jnp.sum(jnp.where(ahead, 1.0, 0.0), axis=1, keepdims=True)
    pair_at = jnp.sum(jnp.where(rank == col.astype(f32), row.astype(f32), 0.0), axis=0, keepdims=True)
    rank_of = jnp.sum(jnp.where(row == col, jnp.broadcast_to(rank, (total, total)), 0.0), axis=0, keepdims=True)
    room = jnp.sum(jnp.where(rank == float(heavy_pairs(H, pairs)), down, 0.0), axis=0, keepdims=True)
    return rank_of, pair_at, room


def survey_body(dims, counts_ref, info_ref, pick_ref, own, others, load, send, recv):
    NP, H, pairs = dims
    total = HEADS // 2
    part = lax.axis_index("parts")
    barrier = pltpu.get_barrier_semaphore()
    for d in range(1, NP):
        pl.semaphore_signal(barrier, inc=1, device_id={"parts": lax.rem(part + d, NP)}, device_id_type=MESH)
    mine = pltpu.make_async_copy(counts_ref, own, load.at[0])
    mine.start()

    def copy(d):
        return pltpu.make_async_remote_copy(
            src_ref=counts_ref,
            dst_ref=others.at[d - 1],
            send_sem=send.at[d - 1],
            recv_sem=recv.at[d - 1],
            device_id={"parts": lax.rem(part + d, NP)},
            device_id_type=MESH,
        )

    pl.semaphore_wait(barrier, NP - 1)
    for d in range(1, NP):
        copy(d).start()
    mine.wait()
    rank_of, pair_at, room = ranked(own, H, pairs)
    info_ref[0:1, :total] = pair_at.astype(jnp.int32)
    info_ref[1:2, :total] = rank_of.astype(jnp.int32)
    for d in range(1, NP):
        copy(d).wait_recv()
        room = jnp.maximum(room, ranked(others.at[d - 1], H, pairs)[2])
    pick = jnp.zeros((1, 1), jnp.int32)
    for less in ROOMS[:-1]:
        pick = pick + (room > float(less)).astype(jnp.int32)
    pick_ref[...] = pick
    for d in range(1, NP):
        copy(d).wait_send()


def survey(counts, NP, H, pairs):
    return pl.pallas_call(
        functools.partial(survey_body, (NP, H, pairs)),
        out_shape=(jax.ShapeDtypeStruct((8, 128), jnp.int32), jax.ShapeDtypeStruct((1, 1), jnp.int32)),
        in_specs=[pl.BlockSpec(memory_space=pltpu.HBM)],
        out_specs=(pl.BlockSpec(memory_space=pltpu.VMEM),) * 2,
        scratch_shapes=[
            pltpu.VMEM(counts.shape, jnp.int32),
            pltpu.VMEM((NP - 1,) + counts.shape, jnp.int32),
            pltpu.SemaphoreType.DMA((1,)),
            pltpu.SemaphoreType.DMA((NP - 1,)),
            pltpu.SemaphoreType.DMA((NP - 1,)),
        ],
        compiler_params=pltpu.CompilerParams(collective_id=0, has_side_effects=True),
        name="survey",
    )(counts)


def slot_ranges(p, c, pairs, room):
    if c == 1 and p == pairs - 1:
        return [(0, MOST), (MOST, room)]
    if p == 0:
        return [(0, 1), (1, room)]
    return [(0, room)]


def body(dims, lists_ref, counts_ref, info_ref, q_ref, k_ref, v_ref, out_ref, *scratch):
    H, S, rows, heads, piece, light = dims
    pairs = heads // 2
    last = pairs - 1
    chips = H // 2
    kb, vb, qb = scratch[: 2 * pairs], scratch[2 * pairs : 4 * pairs], scratch[4 * pairs : 5 * pairs]
    (qin, kin, vin, qs, ks, vs, ob, land, pk, fk, pbuf, mbuf, tbuf, lbuf, lsm, csm, info,
     x_send, x_recv, z_send, z_recv, l_send, l_recv, l_loc, o_send, o_recv) = scratch[5 * pairs :]
    me = lax.axis_index("head")
    tile = lax.axis_index("seq")
    core = lax.rem(me, 2)

    def peer_of(i):
        chip = lax.rem(lax.div(me, 2) + 1 + lax.div(i, 2), chips)
        return chip * 2 + lax.rem(me + i + 1, 2)

    def source_of(i):
        chip = lax.rem(lax.div(me, 2) + 2 * chips - 1 - lax.div(i, 2), chips)
        return chip * 2 + lax.rem(me + i + 1, 2)

    def tile_after(d):
        return lax.rem(tile + d, S)

    def i32(i):
        return jnp.int32(i)

    def with_room(p, what):
        if pairs != 4 or light == PAIR_MOST or p in (0, last):
            what(PAIR_MOST)
        elif p == 1:
            what(light)
        else:
            pl.when(core == 0)(lambda: what(PAIR_MOST))
            pl.when(core != 0)(lambda: what(light))

    scalars = [
        pltpu.make_async_copy(ref, to, l_loc.at[n])
        for n, (ref, to) in enumerate(((info_ref, info), (counts_ref, csm)))
    ]
    inputs = ((k_ref, kin), (v_ref, vin), (q_ref, qin))
    scalars[0].start()
    scalars[1].start()
    for a, (ref, to) in enumerate(inputs):
        for pair in range(HEADS // 2):
            columns = slice(2 * pair * DH, 2 * (pair + 1) * DH)
            pltpu.make_async_copy(ref.at[..., columns], to.at[pair], l_loc.at[2 + a]).start()
    barrier = pltpu.get_barrier_semaphore()
    for d in range(1, S):
        pl.semaphore_signal(barrier, inc=1, device_id={"seq": tile_after(d)}, device_id_type=MESH)
    for i in range(H - 1):
        pl.semaphore_signal(barrier, inc=1, device_id={"head": peer_of(i32(i))}, device_id_type=MESH)

    def pair_of(h, p):
        return info[0, rank_at(H, pairs, h, p)]

    def row_range(owner):
        return pl.ds(pl.multiple_of(owner * rows, 16), rows)

    def piece_range(owner):
        return pl.ds(owner * (rows // piece), rows // piece)

    def staged(a, p, hs, i):
        return qs.at[p, i] if a == 2 else (ks, vs)[a].at[p, hs, i]

    def place_at(a, owner, p, hs):
        if a == 2:
            return qb[p].at[row_range(owner), :]
        return (kb, vb)[a][2 * p + hs].at[piece_range(owner)]

    def x_copy(a, p, hs, i, landed):
        at = source_of(i32(i)) if landed else me
        return pltpu.make_async_remote_copy(
            src_ref=staged(a, p, hs, i),
            dst_ref=place_at(a, at, p, hs),
            send_sem=x_send.at[a],
            recv_sem=x_recv.at[a, p, hs],
            device_id={"head": peer_of(i32(i))},
            device_id_type=MESH,
        )

    def l_copy(d):
        return pltpu.make_async_remote_copy(
            src_ref=lists_ref,
            dst_ref=lbuf.at[d - 1],
            send_sem=l_send.at[0],
            recv_sem=l_recv.at[0],
            device_id={"seq": tile_after(d)},
            device_id_type=MESH,
        )

    def z_copy(p, d, c, g, room):
        lo, hi = slot_ranges(p, c, pairs, room)[g]
        return pltpu.make_async_remote_copy(
            src_ref=pk.at[p, d - 1, c, lo:hi],
            dst_ref=fk.at[p, d - 1, c, lo:hi],
            send_sem=z_send.at[p],
            recv_sem=z_recv.at[p, c, g],
            device_id={"seq": tile_after(d)},
            device_id_type=MESH,
        )

    def o_copy(p, hs, i, landed):
        at = source_of(i) if landed else me
        return pltpu.make_async_remote_copy(
            src_ref=ob.at[p, hs, i],
            dst_ref=land.at[rank_at(H, pairs, at, p), hs],
            send_sem=o_send.at[0],
            recv_sem=o_recv.at[0],
            device_id={"head": peer_of(i)},
            device_id_type=MESH,
        )

    loaded = set()

    def x_start(a, p):
        if a not in loaded:
            loaded.add(a)
            whole = inputs[a][1]
            pltpu.make_async_copy(whole, whole, l_loc.at[2 + a]).wait()
        for hs in range(1 if a == 2 else 2):
            for i in range(H):
                pair = pair_of(peer_of(i32(i)), p)
                if a == 2:
                    taken = qin[pair]
                else:
                    taken = (kin, vin)[a][pair, :, :, hs * DH : (hs + 1) * DH]
                if i < H - 1:
                    staged(a, p, hs, i)[...] = taken
                    x_copy(a, p, hs, i, False).start()
                else:
                    place_at(a, me, p, hs)[...] = taken

    def all_of(ref, send_sem, recv_sem):
        return pltpu.make_async_remote_copy(
            src_ref=ref, dst_ref=ref, send_sem=send_sem, recv_sem=recv_sem,
            device_id={"head": peer_of(i32(0))}, device_id_type=MESH,
        )

    def x_arrived(a, p, hs):
        all_of(qs.at[p] if a == 2 else (ks, vs)[a].at[p, hs], x_send.at[a], x_recv.at[a, p, hs]).wait_recv()

    scalars[0].wait()
    pl.semaphore_wait(barrier, H - 1 + S - 1)
    for d in range(1, S):
        l_copy(d).start()
    order = []
    for p in range(pairs):
        order += [(0, p), (1, p)]
        if p >= 1:
            order.append((2, p - 1))
    order.append((2, last))
    for a, p in order[:4]:
        x_start(a, p)

    scalars[1].wait()
    all_of(lbuf, l_send.at[0], l_recv.at[0]).wait_recv()
    to_scalars = pltpu.make_async_copy(lbuf, lsm, l_loc.at[5])
    to_scalars.start()
    to_scalars.wait()

    waited = set()

    def need(a, p, hs):
        if (a, p, hs) not in waited:
            waited.add((a, p, hs))
            x_arrived(a, p, hs)

    def pack(p, c, g, room):
        held = (kb, vb)[c][2 * p : 2 * p + 2]
        lo, hi = slot_ranges(p, c, pairs, room)[g]
        most = min(MOST, room)
        head = 2 * pair_of(me, p)
        for d in range(1, S):
            at = S - d - 1
            first = csm[tile_after(d), tile, head]
            for s in range(lo, hi):
                left = lsm[at, min(s, MOST - 1), tile, head]
                right = lsm[at, min(room - 1 - s, MOST - 1), tile, head + 1]
                for b in range(BLOCK // piece):
                    if s < most:
                        chosen = held[0][left * (BLOCK // piece) + b]
                    if s >= room - most:
                        other = held[1][right * (BLOCK // piece) + b]
                        chosen = jnp.where(s < first, chosen, other) if s < most else other
                    pk[p, d - 1, c, s, pl.ds(b * piece, piece), :] = chosen
            z_copy(p, d, c, g, room).start()

    def pack_place(p, c):
        if p == 0:
            need(c, p, 0)
            pack(p, c, 0, PAIR_MOST)
            need(c, p, 1)
            for g in range(1, len(slot_ranges(p, c, pairs, PAIR_MOST))):
                pack(p, c, g, PAIR_MOST)
        else:
            need(c, p, 0)
            need(c, p, 1)

            def send(room):
                for g in range(len(slot_ranges(p, c, pairs, room))):
                    pack(p, c, g, room)

            with_room(p, send)

    factor = math.log2(math.e) / math.sqrt(DH)

    def z_arrived(p, c, g, room):
        lo, hi = slot_ranges(p, c, pairs, room)[g]
        all_of(fk.at[p, :, c, lo:hi], z_send.at[p], z_recv.at[p, c, g]).wait_recv()

    def far_slots(hs, room):
        most = min(MOST, room)
        return slice(0, most) if hs == 0 else slice(room - most, room)

    def far_blocks(p, c, d, hs, room):
        return fk[p, d - 1, c, far_slots(hs, room)].reshape(min(MOST, room) * BLOCK, DH)

    def scores_of(p, hs, q, room):
        width = min(MOST, room) * BLOCK
        lane = lax.broadcasted_iota(jnp.int32, (1, width), 1)
        scores = [contract_last(q, kb[2 * p + hs][...].reshape(TILE, DH))]
        head = 2 * pair_of(me, p) + hs
        for d in range(1, S):
            used = csm[tile, lax.rem(tile + S - d, S), head] * BLOCK
            live = lane < used if hs == 0 else lane >= width - used
            bias = jnp.where(live, 0.0, -jnp.inf).astype(jnp.float32)
            scores.append(contract_last(q, far_blocks(p, 0, d, hs, room)) + bias)
        top = functools.reduce(jnp.maximum, [jnp.max(s, axis=1, keepdims=True) for s in scores])
        return scores, top

    def weigh(s, top):
        return jnp.exp2((s - top) * factor)

    def mix(w, v):
        return jnp.dot(w, v, preferred_element_type=jnp.float32)

    def finish(p, hs, i, out):
        ob[p, hs, i] = out

        @pl.when(i < H - 1)
        def _():
            o_copy(p, hs, i, False).start()

    def land_own(p, hs):
        land[rank_at(H, pairs, me, p), hs] = ob[p, hs, H - 1]

    def weigh_place(p):
        def all_chunks(room):
            width = min(MOST, room) * BLOCK
            for g in range(len(slot_ranges(p, 0, pairs, room))):
                z_arrived(p, 0, g, room)

            def chunk(i, carry):
                mine = row_range(peer_of(i))
                for hs in range(2):
                    q = qb[p][mine, hs * DH : (hs + 1) * DH]
                    scores, top = scores_of(p, hs, q, room)
                    w = weigh(scores[0], top)
                    total = jnp.sum(w, axis=1, keepdims=True)
                    mbuf[hs, i] = mix(w.astype(jnp.bfloat16), vb[2 * p + hs][...].reshape(TILE, DH))
                    for d in range(1, S):
                        w = weigh(scores[d], top)
                        total = total + jnp.sum(w, axis=1, keepdims=True)
                        pbuf[hs, i, :, (d - 1) * width : d * width] = w.astype(jnp.bfloat16)
                    tbuf[hs, i] = total
                return carry

            lax.fori_loop(0, H, chunk, 0)

        need(2, p, 0)
        with_room(p, all_chunks)

    def mix_place(p):
        def all_chunks(room):
            width = min(MOST, room) * BLOCK
            groups = len(slot_ranges(p, 1, pairs, room))
            for hs in range(2):
                for g in range(groups) if p < last and hs == 0 else range(hs, hs + 1) if p == last else ():
                    z_arrived(p, 1, g, room)

                def chunk(i, carry, hs=hs):
                    mixed = mbuf[hs, i]
                    for d in range(1, S):
                        weights = pbuf[hs, i, :, (d - 1) * width : d * width]
                        mixed = mixed + mix(weights, far_blocks(p, 1, d, hs, room))
                    finish(p, hs, i, (mixed / tbuf[hs, i]).astype(jnp.bfloat16))
                    return carry

                lax.fori_loop(0, H, chunk, 0)
                land_own(p, hs)

        with_room(p, all_chunks)

    pack_place(0, 0)
    pack_place(0, 1)
    for a, p in order[4:]:
        x_start(a, p)
    for p in range(1, last):
        pack_place(p, 0)
        pack_place(p, 1)
    for p in range(pairs):
        weigh_place(p)
        mix_place(p)
        if last > 0 and p < 2:
            for c in range(2) if last == 1 else (p,):
                if p < last:
                    pack_place(last, c)

    sent_out = all_of(ob.at[:, :, : H - 1], o_send.at[0], o_recv.at[0])
    sent_out.wait_recv()
    for pair in range(HEADS // 2):
        rank = info[1, pair]
        for hs in range(2):
            out_ref[:, (2 * pair + hs) * DH : (2 * pair + hs + 1) * DH] = land[rank, hs]
    all_of(lbuf, l_send.at[0], l_recv.at[0]).wait_send()
    for p in range(pairs):

        def sent(room, p=p):
            all_of(pk.at[p, :, :, :room], z_send.at[p], z_recv.at[p, 0, 0]).wait_send()

        with_room(p, sent)
    for a, ref in enumerate((ks, vs, qs)):
        all_of(ref, x_send.at[a], x_recv.at[a, 0, 0]).wait_send()
    sent_out.wait_send()


def attention(dims, number, lists, counts, info, query_rows, key_rows, value_rows):
    H, S, rows, heads, piece, light = dims
    pairs = heads // 2
    bf16 = jnp.bfloat16
    chunk = (rows // piece, piece, query_rows.shape[1])
    operands = (lists, counts, info, query_rows, key_rows.reshape(chunk), value_rows.reshape(chunk))
    return pl.pallas_call(
        functools.partial(body, dims),
        out_shape=pltpu.VMEM(query_rows.shape, bf16),
        in_specs=[pl.BlockSpec(memory_space=pltpu.HBM)] * 6,
        out_specs=pl.BlockSpec(memory_space=pltpu.VMEM),
        scratch_shapes=[pltpu.VMEM((TILE // piece, piece, DH), bf16) for _ in range(4 * pairs)]
        + [pltpu.VMEM((TILE, 2 * DH), bf16) for _ in range(pairs)]
        + [
            pltpu.VMEM((HEADS // 2, rows, 2 * DH), bf16),
            pltpu.VMEM((HEADS // 2, rows // piece, piece, 2 * DH), bf16),
            pltpu.VMEM((HEADS // 2, rows // piece, piece, 2 * DH), bf16),
            pltpu.VMEM((pairs, H - 1, rows, 2 * DH), bf16),
            pltpu.VMEM((pairs, 2, H - 1, rows // piece, piece, DH), bf16),
            pltpu.VMEM((pairs, 2, H - 1, rows // piece, piece, DH), bf16),
            pltpu.VMEM((pairs, 2, H, rows, DH), bf16),
            pltpu.VMEM((HEADS // 2, 2, rows, DH), bf16),
            pltpu.VMEM((pairs, S - 1, 2, PAIR_MOST, BLOCK, DH), bf16),
            pltpu.VMEM((pairs, S - 1, 2, PAIR_MOST, BLOCK, DH), bf16),
            pltpu.VMEM((2, H, rows, (S - 1) * MOST * BLOCK), bf16),
            pltpu.VMEM((2, H, rows, DH), jnp.float32),
            pltpu.VMEM((2, H, rows, 1), jnp.float32),
            pltpu.VMEM((S - 1,) + lists.shape, jnp.int32),
            pltpu.SMEM((S - 1,) + lists.shape, jnp.int32),
            pltpu.SMEM(counts.shape, jnp.int32),
            pltpu.SMEM((8, 128), jnp.int32),
            pltpu.SemaphoreType.DMA((3,)),
            pltpu.SemaphoreType.DMA((3, pairs, 2)),
            pltpu.SemaphoreType.DMA((pairs,)),
            pltpu.SemaphoreType.DMA((pairs, 2, 2)),
            pltpu.SemaphoreType.DMA((1,)),
            pltpu.SemaphoreType.DMA((1,)),
            pltpu.SemaphoreType.DMA((6,)),
            pltpu.SemaphoreType.DMA((1,)),
            pltpu.SemaphoreType.DMA((1,)),
        ],
        compiler_params=pltpu.CompilerParams(
            collective_id=number, has_side_effects=True, vmem_limit_bytes=VMEM_LIMIT
        ),
        name=f"block_attention_{light}",
    )(*operands)


def on_device(query_rows, key_rows, value_rows, block_lists, block_counts):
    H = lax.axis_size("head")
    S = lax.axis_size("seq")
    rows = query_rows.shape[0]
    heads = HEADS // H
    pairs = heads // 2
    lists = jnp.transpose(block_lists, (1, 3, 2, 0))[0]
    counts = jnp.transpose(block_counts, (1, 2, 0))
    piece = math.gcd(rows, BLOCK)
    rooms = ROOMS if pairs == 4 else (PAIR_MOST,)
    kernels = [
        functools.partial(attention, (H, S, rows, heads, piece, room), 1 + n) for n, room in enumerate(rooms)
    ]
    if len(rooms) == 1:
        info = jnp.broadcast_to(jnp.arange(128, dtype=jnp.int32), (8, 128))
        return kernels[0](lists, counts, info, query_rows, key_rows, value_rows)
    info, pick = survey(counts, lax.axis_size("parts"), H, pairs)
    return lax.switch(pick[0, 0], kernels, lists, counts, info, query_rows, key_rows, value_rows)


def solution(mesh):
    in_specs = (
        P(("parts", "seq", "head"), None),
        P(("parts", "seq", "head"), None),
        P(("parts", "seq", "head"), None),
        P("parts", "seq", None, None),
        P("parts", None, None),
    )
    out_specs = P(("parts", "seq", "head"), None)
    return jax.shard_map(
        on_device, mesh=mesh, in_specs=in_specs, out_specs=out_specs, check_vma=False
    )
```

```python
import functools
import math

import jax
import jax.numpy as jnp
from jax import lax
from jax.experimental import pallas as pl
from jax.experimental.pallas import tpu as pltpu
from jax.sharding import PartitionSpec as P

HEADS = 32
DH = 128
BLOCK = 128
MOST = 3
PAIR_MOST = 4
TILE = 768
MESH = pl.DeviceIdType.MESH
ROOMS = (1, PAIR_MOST)
VMEM_LIMIT = 60 << 20


def contract_last(a, b):
    return lax.dot_general(a, b, (((1,), (1,)), ((), ())), preferred_element_type=jnp.float32)


def rank_at(H, pairs, h, p):
    if pairs != 4:
        return p * H + h
    chips = H // 2
    if p == 2:
        return 2 * H + lax.rem(h, 2) * chips + lax.div(h, 2)
    return {0: 0, 1: 3 * H, 3: H}[p] + h


def heavy_pairs(H, pairs):
    return 2 * H + H // 2 if pairs == 4 else H * pairs


def ranked(counts, H, pairs):
    total = HEADS // 2
    f32 = jnp.float32
    head_no = lax.broadcasted_iota(jnp.int32, (HEADS, total), 0)
    pair_no = lax.broadcasted_iota(jnp.int32, (HEADS, total), 1)
    in_pair = jnp.where((head_no == 2 * pair_no) | (head_no == 2 * pair_no + 1), 1.0, 0.0).astype(f32)
    most = jnp.zeros((1, total), f32)
    for t in range(counts.shape[0]):
        sums = jnp.dot(counts[t].astype(f32), in_pair, preferred_element_type=f32)
        most = jnp.maximum(most, jnp.max(sums, axis=0, keepdims=True))
    row = lax.broadcasted_iota(jnp.int32, (total, total), 0)
    col = lax.broadcasted_iota(jnp.int32, (total, total), 1)
    along = jnp.broadcast_to(most, (total, total))
    down = jnp.sum(jnp.where(row == col, along, 0.0), axis=1, keepdims=True)
    ahead = (along > down) | ((along == down) & (col < row))
    rank = jnp.sum(jnp.where(ahead, 1.0, 0.0), axis=1, keepdims=True)
    pair_at = jnp.sum(jnp.where(rank == col.astype(f32), row.astype(f32), 0.0), axis=0, keepdims=True)
    rank_of = jnp.sum(jnp.where(row == col, jnp.broadcast_to(rank, (total, total)), 0.0), axis=0, keepdims=True)
    room = jnp.sum(jnp.where(rank == float(heavy_pairs(H, pairs)), down, 0.0), axis=0, keepdims=True)
    return rank_of, pair_at, room


def survey_body(dims, counts_ref, info_ref, pick_ref, own, others, load, send, recv):
    NP, H, pairs = dims
    total = HEADS // 2
    part = lax.axis_index("parts")
    barrier = pltpu.get_barrier_semaphore()
    for d in range(1, NP):
        pl.semaphore_signal(barrier, inc=1, device_id={"parts": lax.rem(part + d, NP)}, device_id_type=MESH)
    mine = pltpu.make_async_copy(counts_ref, own, load.at[0])
    mine.start()

    def copy(d):
        return pltpu.make_async_remote_copy(
            src_ref=counts_ref,
            dst_ref=others.at[d - 1],
            send_sem=send.at[d - 1],
            recv_sem=recv.at[d - 1],
            device_id={"parts": lax.rem(part + d, NP)},
            device_id_type=MESH,
        )

    pl.semaphore_wait(barrier, NP - 1)
    for d in range(1, NP):
        copy(d).start()
    mine.wait()
    rank_of, pair_at, room = ranked(own, H, pairs)
    info_ref[0:1, :total] = pair_at.astype(jnp.int32)
    info_ref[1:2, :total] = rank_of.astype(jnp.int32)
    for d in range(1, NP):
        copy(d).wait_recv()
        room = jnp.maximum(room, ranked(others.at[d - 1], H, pairs)[2])
    pick = jnp.zeros((1, 1), jnp.int32)
    for less in ROOMS[:-1]:
        pick = pick + (room > float(less)).astype(jnp.int32)
    pick_ref[...] = pick
    for d in range(1, NP):
        copy(d).wait_send()


def survey(counts, NP, H, pairs):
    return pl.pallas_call(
        functools.partial(survey_body, (NP, H, pairs)),
        out_shape=(jax.ShapeDtypeStruct((8, 128), jnp.int32), jax.ShapeDtypeStruct((1, 1), jnp.int32)),
        in_specs=[pl.BlockSpec(memory_space=pltpu.HBM)],
        out_specs=(pl.BlockSpec(memory_space=pltpu.VMEM),) * 2,
        scratch_shapes=[
            pltpu.VMEM(counts.shape, jnp.int32),
            pltpu.VMEM((NP - 1,) + counts.shape, jnp.int32),
            pltpu.SemaphoreType.DMA((1,)),
            pltpu.SemaphoreType.DMA((NP - 1,)),
            pltpu.SemaphoreType.DMA((NP - 1,)),
        ],
        compiler_params=pltpu.CompilerParams(collective_id=0, has_side_effects=True),
        name="survey",
    )(counts)


def slot_ranges(p, c, pairs, room):
    if c == 1 and p == pairs - 1:
        return [(0, MOST), (MOST, room)]
    if p == 0:
        return [(0, 1), (1, room)]
    return [(0, room)]


def body(dims, lists_ref, counts_ref, info_ref, q_ref, k_ref, v_ref, out_ref, *scratch):
    H, S, rows, heads, piece, light = dims
    pairs = heads // 2
    last = pairs - 1
    chips = H // 2
    kb, vb, qb = scratch[: 2 * pairs], scratch[2 * pairs : 4 * pairs], scratch[4 * pairs : 5 * pairs]
    (qin, kin, vin, qs, ks, vs, ob, land, pk, fk, pbuf, mbuf, tbuf, lbuf, lsm, csm, info,
     x_send, x_recv, z_send, z_recv, l_send, l_recv, l_loc, o_send, o_recv) = scratch[5 * pairs :]
    me = lax.axis_index("head")
    tile = lax.axis_index("seq")
    core = lax.rem(me, 2)

    def peer_of(i):
        chip = lax.rem(lax.div(me, 2) + 1 + lax.div(i, 2), chips)
        return chip * 2 + lax.rem(me + i + 1, 2)

    def source_of(i):
        chip = lax.rem(lax.div(me, 2) + 2 * chips - 1 - lax.div(i, 2), chips)
        return chip * 2 + lax.rem(me + i + 1, 2)

    def tile_after(d):
        return lax.rem(tile + d, S)

    def i32(i):
        return jnp.int32(i)

    def with_room(p, what):
        if pairs != 4 or light == PAIR_MOST or p in (0, last):
            what(PAIR_MOST)
        elif p == 1:
            what(light)
        else:
            pl.when(core == 0)(lambda: what(PAIR_MOST))
            pl.when(core != 0)(lambda: what(light))

    scalars = [
        pltpu.make_async_copy(ref, to, l_loc.at[n])
        for n, (ref, to) in enumerate(((info_ref, info), (counts_ref, csm)))
    ]
    inputs = ((k_ref, kin), (v_ref, vin), (q_ref, qin))
    scalars[0].start()
    scalars[1].start()
    for a, (ref, to) in enumerate(inputs):
        for pair in range(HEADS // 2):
            columns = slice(2 * pair * DH, 2 * (pair + 1) * DH)
            pltpu.make_async_copy(ref.at[..., columns], to.at[pair], l_loc.at[2 + a]).start()
    barrier = pltpu.get_barrier_semaphore()
    for d in range(1, S):
        pl.semaphore_signal(barrier, inc=1, device_id={"seq": tile_after(d)}, device_id_type=MESH)
    for i in range(H - 1):
        pl.semaphore_signal(barrier, inc=1, device_id={"head": peer_of(i32(i))}, device_id_type=MESH)

    def pair_of(h, p):
        return info[0, rank_at(H, pairs, h, p)]

    def row_range(owner):
        return pl.ds(pl.multiple_of(owner * rows, 16), rows)

    def piece_range(owner):
        return pl.ds(owner * (rows // piece), rows // piece)

    def staged(a, p, hs, i):
        return qs.at[p, i] if a == 2 else (ks, vs)[a].at[p, hs, i]

    def place_at(a, owner, p, hs):
        if a == 2:
            return qb[p].at[row_range(owner), :]
        return (kb, vb)[a][2 * p + hs].at[piece_range(owner)]

    def x_copy(a, p, hs, i, landed):
        at = source_of(i32(i)) if landed else me
        return pltpu.make_async_remote_copy(
            src_ref=staged(a, p, hs, i),
            dst_ref=place_at(a, at, p, hs),
            send_sem=x_send.at[a],
            recv_sem=x_recv.at[a, p, hs],
            device_id={"head": peer_of(i32(i))},
            device_id_type=MESH,
        )

    def l_copy(d):
        return pltpu.make_async_remote_copy(
            src_ref=lists_ref,
            dst_ref=lbuf.at[d - 1],
            send_sem=l_send.at[0],
            recv_sem=l_recv.at[0],
            device_id={"seq": tile_after(d)},
            device_id_type=MESH,
        )

    def z_copy(p, d, c, g, room):
        lo, hi = slot_ranges(p, c, pairs, room)[g]
        return pltpu.make_async_remote_copy(
            src_ref=pk.at[p, d - 1, c, lo:hi],
            dst_ref=fk.at[p, d - 1, c, lo:hi],
            send_sem=z_send.at[p],
            recv_sem=z_recv.at[p, c, g],
            device_id={"seq": tile_after(d)},
            device_id_type=MESH,
        )

    def o_copy(p, hs, i, landed):
        at = source_of(i) if landed else me
        return pltpu.make_async_remote_copy(
            src_ref=ob.at[p, hs, i],
            dst_ref=land.at[rank_at(H, pairs, at, p), hs],
            send_sem=o_send.at[0],
            recv_sem=o_recv.at[0],
            device_id={"head": peer_of(i)},
            device_id_type=MESH,
        )

    loaded = set()

    def x_start(a, p):
        if a not in loaded:
            loaded.add(a)
            whole = inputs[a][1]
            pltpu.make_async_copy(whole, whole, l_loc.at[2 + a]).wait()
        for hs in range(1 if a == 2 else 2):
            for i in range(H):
                pair = pair_of(peer_of(i32(i)), p)
                if a == 2:
                    taken = qin[pair]
                else:
                    taken = (kin, vin)[a][pair, :, :, hs * DH : (hs + 1) * DH]
                if i < H - 1:
                    staged(a, p, hs, i)[...] = taken
                    x_copy(a, p, hs, i, False).start()
                else:
                    place_at(a, me, p, hs)[...] = taken

    def all_of(ref, send_sem, recv_sem):
        return pltpu.make_async_remote_copy(
            src_ref=ref, dst_ref=ref, send_sem=send_sem, recv_sem=recv_sem,
            device_id={"head": peer_of(i32(0))}, device_id_type=MESH,
        )

    def x_arrived(a, p, hs):
        all_of(qs.at[p] if a == 2 else (ks, vs)[a].at[p, hs], x_send.at[a], x_recv.at[a, p, hs]).wait_recv()

    scalars[0].wait()
    pl.semaphore_wait(barrier, H - 1 + S - 1)
    for d in range(1, S):
        l_copy(d).start()
    if pairs == 4:
        order = [(0, 0), (1, 0), (0, 1), (1, 1), (2, 0), (0, 2), (0, 3), (1, 2), (2, 1), (2, 2), (1, 3), (2, 3)]
    else:
        order = [(a, p) for p in range(pairs) for a in range(3)]
    for a, p in order[:4]:
        x_start(a, p)

    scalars[1].wait()
    all_of(lbuf, l_send.at[0], l_recv.at[0]).wait_recv()
    to_scalars = pltpu.make_async_copy(lbuf, lsm, l_loc.at[5])
    to_scalars.start()
    to_scalars.wait()

    waited = set()

    def need(a, p, hs):
        if (a, p, hs) not in waited:
            waited.add((a, p, hs))
            x_arrived(a, p, hs)

    def pack(p, c, g, room):
        held = (kb, vb)[c][2 * p : 2 * p + 2]
        lo, hi = slot_ranges(p, c, pairs, room)[g]
        most = min(MOST, room)
        head = 2 * pair_of(me, p)
        for d in range(1, S):
            at = S - d - 1
            first = csm[tile_after(d), tile, head]
            for s in range(lo, hi):
                left = lsm[at, min(s, MOST - 1), tile, head]
                right = lsm[at, min(room - 1 - s, MOST - 1), tile, head + 1]
                for b in range(BLOCK // piece):
                    if s < most:
                        chosen = held[0][left * (BLOCK // piece) + b]
                    if s >= room - most:
                        other = held[1][right * (BLOCK // piece) + b]
                        chosen = jnp.where(s < first, chosen, other) if s < most else other
                    pk[p, d - 1, c, s, pl.ds(b * piece, piece), :] = chosen
            z_copy(p, d, c, g, room).start()

    def pack_place(p, c):
        if p == 0:
            need(c, p, 0)
            pack(p, c, 0, PAIR_MOST)
            need(c, p, 1)
            for g in range(1, len(slot_ranges(p, c, pairs, PAIR_MOST))):
                pack(p, c, g, PAIR_MOST)
        else:
            need(c, p, 0)
            need(c, p, 1)

            def send(room):
                for g in range(len(slot_ranges(p, c, pairs, room))):
                    pack(p, c, g, room)

            with_room(p, send)

    factor = math.log2(math.e) / math.sqrt(DH)

    def z_arrived(p, c, g, room):
        lo, hi = slot_ranges(p, c, pairs, room)[g]
        all_of(fk.at[p, :, c, lo:hi], z_send.at[p], z_recv.at[p, c, g]).wait_recv()

    def far_slots(hs, room):
        most = min(MOST, room)
        return slice(0, most) if hs == 0 else slice(room - most, room)

    def far_blocks(p, c, d, hs, room):
        return fk[p, d - 1, c, far_slots(hs, room)].reshape(min(MOST, room) * BLOCK, DH)

    def scores_of(p, hs, q, room):
        width = min(MOST, room) * BLOCK
        lane = lax.broadcasted_iota(jnp.int32, (1, width), 1)
        scores = [contract_last(q, kb[2 * p + hs][...].reshape(TILE, DH))]
        head = 2 * pair_of(me, p) + hs
        for d in range(1, S):
            used = csm[tile, lax.rem(tile + S - d, S), head] * BLOCK
            live = lane < used if hs == 0 else lane >= width - used
            bias = jnp.where(live, 0.0, -jnp.inf).astype(jnp.float32)
            scores.append(contract_last(q, far_blocks(p, 0, d, hs, room)) + bias)
        top = functools.reduce(jnp.maximum, [jnp.max(s, axis=1, keepdims=True) for s in scores])
        return scores, top

    def weigh(s, top):
        return jnp.exp2((s - top) * factor)

    def mix(w, v):
        return jnp.dot(w, v, preferred_element_type=jnp.float32)

    def finish(p, hs, i, out):
        ob[p, hs, i] = out

        @pl.when(i < H - 1)
        def _():
            o_copy(p, hs, i, False).start()

    def land_own(p, hs):
        land[rank_at(H, pairs, me, p), hs] = ob[p, hs, H - 1]

    def weigh_place(p):
        def all_chunks(room):
            width = min(MOST, room) * BLOCK
            for g in range(len(slot_ranges(p, 0, pairs, room))):
                z_arrived(p, 0, g, room)

            def chunk(i, carry):
                mine = row_range(peer_of(i))
                for hs in range(2):
                    q = qb[p][mine, hs * DH : (hs + 1) * DH]
                    scores, top = scores_of(p, hs, q, room)
                    w = weigh(scores[0], top)
                    total = jnp.sum(w, axis=1, keepdims=True)
                    mbuf[p % 2, hs, i] = mix(w.astype(jnp.bfloat16), vb[2 * p + hs][...].reshape(TILE, DH))
                    for d in range(1, S):
                        w = weigh(scores[d], top)
                        total = total + jnp.sum(w, axis=1, keepdims=True)
                        pbuf[p % 2, hs, i, :, (d - 1) * width : d * width] = w.astype(jnp.bfloat16)
                    tbuf[p % 2, hs, i] = total
                return carry

            lax.fori_loop(0, H, chunk, 0)

        need(2, p, 0)
        with_room(p, all_chunks)

    def mix_place(p):
        def all_chunks(room):
            width = min(MOST, room) * BLOCK
            groups = len(slot_ranges(p, 1, pairs, room))
            for hs in range(2):
                for g in range(groups) if p < last and hs == 0 else range(hs, hs + 1) if p == last else ():
                    z_arrived(p, 1, g, room)

                def chunk(i, carry, hs=hs):
                    mixed = mbuf[p % 2, hs, i]
                    for d in range(1, S):
                        weights = pbuf[p % 2, hs, i, :, (d - 1) * width : d * width]
                        mixed = mixed + mix(weights, far_blocks(p, 1, d, hs, room))
                    finish(p, hs, i, (mixed / tbuf[p % 2, hs, i]).astype(jnp.bfloat16))
                    return carry

                lax.fori_loop(0, H, chunk, 0)
                land_own(p, hs)

        with_room(p, all_chunks)

    pack_place(0, 0)
    pack_place(0, 1)
    for a, p in order[4:]:
        x_start(a, p)
    if pairs == 4:
        pack_place(1, 0)
        pack_place(1, 1)
        pack_place(2, 0)
        pack_place(3, 0)
        weigh_place(0)
        mix_place(0)
        pack_place(2, 1)
        weigh_place(1)
        mix_place(1)
        weigh_place(2)
        pack_place(3, 1)
        weigh_place(3)
        mix_place(2)
        mix_place(3)
    else:
        for p in range(1, pairs):
            pack_place(p, 0)
            pack_place(p, 1)
        for p in range(pairs):
            weigh_place(p)
            mix_place(p)

    sent_out = all_of(ob.at[:, :, : H - 1], o_send.at[0], o_recv.at[0])
    sent_out.wait_recv()
    for pair in range(HEADS // 2):
        rank = info[1, pair]
        for hs in range(2):
            out_ref[:, (2 * pair + hs) * DH : (2 * pair + hs + 1) * DH] = land[rank, hs]
    all_of(lbuf, l_send.at[0], l_recv.at[0]).wait_send()
    for p in range(pairs):

        def sent(room, p=p):
            all_of(pk.at[p, :, :, :room], z_send.at[p], z_recv.at[p, 0, 0]).wait_send()

        with_room(p, sent)
    for a, ref in enumerate((ks, vs, qs)):
        all_of(ref, x_send.at[a], x_recv.at[a, 0, 0]).wait_send()
    sent_out.wait_send()


def attention(dims, number, lists, counts, info, query_rows, key_rows, value_rows):
    H, S, rows, heads, piece, light = dims
    pairs = heads // 2
    bf16 = jnp.bfloat16
    chunk = (rows // piece, piece, query_rows.shape[1])
    operands = (lists, counts, info, query_rows, key_rows.reshape(chunk), value_rows.reshape(chunk))
    return pl.pallas_call(
        functools.partial(body, dims),
        out_shape=pltpu.VMEM(query_rows.shape, bf16),
        in_specs=[pl.BlockSpec(memory_space=pltpu.HBM)] * 6,
        out_specs=pl.BlockSpec(memory_space=pltpu.VMEM),
        scratch_shapes=[pltpu.VMEM((TILE // piece, piece, DH), bf16) for _ in range(4 * pairs)]
        + [pltpu.VMEM((TILE, 2 * DH), bf16) for _ in range(pairs)]
        + [
            pltpu.VMEM((HEADS // 2, rows, 2 * DH), bf16),
            pltpu.VMEM((HEADS // 2, rows // piece, piece, 2 * DH), bf16),
            pltpu.VMEM((HEADS // 2, rows // piece, piece, 2 * DH), bf16),
            pltpu.VMEM((pairs, H - 1, rows, 2 * DH), bf16),
            pltpu.VMEM((pairs, 2, H - 1, rows // piece, piece, DH), bf16),
            pltpu.VMEM((pairs, 2, H - 1, rows // piece, piece, DH), bf16),
            pltpu.VMEM((pairs, 2, H, rows, DH), bf16),
            pltpu.VMEM((HEADS // 2, 2, rows, DH), bf16),
            pltpu.VMEM((pairs, S - 1, 2, PAIR_MOST, BLOCK, DH), bf16),
            pltpu.VMEM((pairs, S - 1, 2, PAIR_MOST, BLOCK, DH), bf16),
            pltpu.VMEM((min(2, pairs), 2, H, rows, (S - 1) * MOST * BLOCK), bf16),
            pltpu.VMEM((min(2, pairs), 2, H, rows, DH), jnp.float32),
            pltpu.VMEM((min(2, pairs), 2, H, rows, 1), jnp.float32),
            pltpu.VMEM((S - 1,) + lists.shape, jnp.int32),
            pltpu.SMEM((S - 1,) + lists.shape, jnp.int32),
            pltpu.SMEM(counts.shape, jnp.int32),
            pltpu.SMEM((8, 128), jnp.int32),
            pltpu.SemaphoreType.DMA((3,)),
            pltpu.SemaphoreType.DMA((3, pairs, 2)),
            pltpu.SemaphoreType.DMA((pairs,)),
            pltpu.SemaphoreType.DMA((pairs, 2, 2)),
            pltpu.SemaphoreType.DMA((1,)),
            pltpu.SemaphoreType.DMA((1,)),
            pltpu.SemaphoreType.DMA((6,)),
            pltpu.SemaphoreType.DMA((1,)),
            pltpu.SemaphoreType.DMA((1,)),
        ],
        compiler_params=pltpu.CompilerParams(
            collective_id=number, has_side_effects=True, vmem_limit_bytes=VMEM_LIMIT
        ),
        name=f"block_attention_{light}",
    )(*operands)


def on_device(query_rows, key_rows, value_rows, block_lists, block_counts):
    H = lax.axis_size("head")
    S = lax.axis_size("seq")
    rows = query_rows.shape[0]
    heads = HEADS // H
    pairs = heads // 2
    lists = jnp.transpose(block_lists, (1, 3, 2, 0))[0]
    counts = jnp.transpose(block_counts, (1, 2, 0))
    piece = math.gcd(rows, BLOCK)
    rooms = ROOMS if pairs == 4 else (PAIR_MOST,)
    kernels = [
        functools.partial(attention, (H, S, rows, heads, piece, room), 1 + n) for n, room in enumerate(rooms)
    ]
    if len(rooms) == 1:
        info = jnp.broadcast_to(jnp.arange(128, dtype=jnp.int32), (8, 128))
        return kernels[0](lists, counts, info, query_rows, key_rows, value_rows)
    info, pick = survey(counts, lax.axis_size("parts"), H, pairs)
    return lax.switch(pick[0, 0], kernels, lists, counts, info, query_rows, key_rows, value_rows)


def solution(mesh):
    in_specs = (
        P(("parts", "seq", "head"), None),
        P(("parts", "seq", "head"), None),
        P(("parts", "seq", "head"), None),
        P("parts", "seq", None, None),
        P("parts", None, None),
    )
    out_specs = P(("parts", "seq", "head"), None)
    return jax.shard_map(
        on_device, mesh=mesh, in_specs=in_specs, out_specs=out_specs, check_vma=False
    )
```

```python
import functools
import math

import jax
import jax.numpy as jnp
from jax import lax
from jax.experimental import pallas as pl
from jax.experimental.pallas import tpu as pltpu
from jax.sharding import PartitionSpec as P

HEADS = 32
DH = 128
BLOCK = 128
MOST = 3
PAIR_MOST = 4
TILE = 768
MESH = pl.DeviceIdType.MESH
ROOMS = (1, 2, PAIR_MOST)
VMEM_LIMIT = 60 << 20


def contract_last(a, b):
    return lax.dot_general(a, b, (((1,), (1,)), ((), ())), preferred_element_type=jnp.float32)


def rank_at(H, pairs, h, p):
    if pairs != 4:
        return p * H + h
    chips = H // 2
    if p == 2:
        return 2 * H + lax.rem(h, 2) * chips + lax.div(h, 2)
    return {0: 0, 1: 3 * H, 3: H}[p] + h


def heavy_pairs(H, pairs):
    return 2 * H + H // 2 if pairs == 4 else H * pairs


def ranked(counts, H, pairs):
    total = HEADS // 2
    f32 = jnp.float32
    head_no = lax.broadcasted_iota(jnp.int32, (HEADS, total), 0)
    pair_no = lax.broadcasted_iota(jnp.int32, (HEADS, total), 1)
    in_pair = jnp.where((head_no == 2 * pair_no) | (head_no == 2 * pair_no + 1), 1.0, 0.0).astype(f32)
    most = jnp.zeros((1, total), f32)
    for t in range(counts.shape[0]):
        sums = jnp.dot(counts[t].astype(f32), in_pair, preferred_element_type=f32)
        most = jnp.maximum(most, jnp.max(sums, axis=0, keepdims=True))
    row = lax.broadcasted_iota(jnp.int32, (total, total), 0)
    col = lax.broadcasted_iota(jnp.int32, (total, total), 1)
    along = jnp.broadcast_to(most, (total, total))
    down = jnp.sum(jnp.where(row == col, along, 0.0), axis=1, keepdims=True)
    ahead = (along > down) | ((along == down) & (col < row))
    rank = jnp.sum(jnp.where(ahead, 1.0, 0.0), axis=1, keepdims=True)
    pair_at = jnp.sum(jnp.where(rank == col.astype(f32), row.astype(f32), 0.0), axis=0, keepdims=True)
    rank_of = jnp.sum(jnp.where(row == col, jnp.broadcast_to(rank, (total, total)), 0.0), axis=0, keepdims=True)
    room = jnp.sum(jnp.where(rank == float(heavy_pairs(H, pairs)), down, 0.0), axis=0, keepdims=True)
    return rank_of, pair_at, room


def survey_body(dims, counts_ref, info_ref, pick_ref, own, others, load, send, recv):
    NP, H, pairs = dims
    total = HEADS // 2
    part = lax.axis_index("parts")
    barrier = pltpu.get_barrier_semaphore()
    for d in range(1, NP):
        pl.semaphore_signal(barrier, inc=1, device_id={"parts": lax.rem(part + d, NP)}, device_id_type=MESH)
    mine = pltpu.make_async_copy(counts_ref, own, load.at[0])
    mine.start()

    def copy(d):
        return pltpu.make_async_remote_copy(
            src_ref=counts_ref,
            dst_ref=others.at[d - 1],
            send_sem=send.at[d - 1],
            recv_sem=recv.at[d - 1],
            device_id={"parts": lax.rem(part + d, NP)},
            device_id_type=MESH,
        )

    pl.semaphore_wait(barrier, NP - 1)
    for d in range(1, NP):
        copy(d).start()
    mine.wait()
    rank_of, pair_at, room = ranked(own, H, pairs)
    info_ref[0:1, :total] = pair_at.astype(jnp.int32)
    info_ref[1:2, :total] = rank_of.astype(jnp.int32)
    for d in range(1, NP):
        copy(d).wait_recv()
        room = jnp.maximum(room, ranked(others.at[d - 1], H, pairs)[2])
    pick = jnp.zeros((1, 1), jnp.int32)
    for less in ROOMS[:-1]:
        pick = pick + (room > float(less)).astype(jnp.int32)
    pick_ref[...] = pick
    for d in range(1, NP):
        copy(d).wait_send()


def survey(counts, NP, H, pairs):
    return pl.pallas_call(
        functools.partial(survey_body, (NP, H, pairs)),
        out_shape=(jax.ShapeDtypeStruct((8, 128), jnp.int32), jax.ShapeDtypeStruct((1, 1), jnp.int32)),
        in_specs=[pl.BlockSpec(memory_space=pltpu.HBM)],
        out_specs=(pl.BlockSpec(memory_space=pltpu.VMEM),) * 2,
        scratch_shapes=[
            pltpu.VMEM(counts.shape, jnp.int32),
            pltpu.VMEM((NP - 1,) + counts.shape, jnp.int32),
            pltpu.SemaphoreType.DMA((1,)),
            pltpu.SemaphoreType.DMA((NP - 1,)),
            pltpu.SemaphoreType.DMA((NP - 1,)),
        ],
        compiler_params=pltpu.CompilerParams(collective_id=0, has_side_effects=True),
        name="survey",
    )(counts)


def slot_ranges(p, c, pairs, room):
    if c == 1 and p == pairs - 1:
        return [(0, MOST), (MOST, room)]
    if p == 0:
        return [(0, 1), (1, room)]
    return [(0, room)]


def body(dims, lists_ref, counts_ref, info_ref, q_ref, k_ref, v_ref, out_ref, *scratch):
    H, S, rows, heads, piece, light = dims
    pairs = heads // 2
    last = pairs - 1
    chips = H // 2
    kb, vb, qb = scratch[: 2 * pairs], scratch[2 * pairs : 4 * pairs], scratch[4 * pairs : 5 * pairs]
    (qin, kin, vin, qs, ks, vs, ob, land, pk, fk, pbuf, mbuf, tbuf, lbuf, lsm, csm, info,
     x_send, x_recv, z_send, z_recv, l_send, l_recv, l_loc, o_send, o_recv) = scratch[5 * pairs :]
    me = lax.axis_index("head")
    tile = lax.axis_index("seq")
    core = lax.rem(me, 2)

    def peer_of(i):
        chip = lax.rem(lax.div(me, 2) + 1 + lax.div(i, 2), chips)
        return chip * 2 + lax.rem(me + i + 1, 2)

    def source_of(i):
        chip = lax.rem(lax.div(me, 2) + 2 * chips - 1 - lax.div(i, 2), chips)
        return chip * 2 + lax.rem(me + i + 1, 2)

    def tile_after(d):
        return lax.rem(tile + d, S)

    def i32(i):
        return jnp.int32(i)

    def with_room(p, what):
        if pairs != 4 or light == PAIR_MOST or p in (0, last):
            what(PAIR_MOST)
        elif p == 1:
            what(light)
        else:
            pl.when(core == 0)(lambda: what(PAIR_MOST))
            pl.when(core != 0)(lambda: what(light))

    barrier = pltpu.get_barrier_semaphore()
    for d in range(1, S):
        pl.semaphore_signal(barrier, inc=1, device_id={"seq": tile_after(d)}, device_id_type=MESH)
    for i in range(H - 1):
        pl.semaphore_signal(barrier, inc=1, device_id={"head": peer_of(i32(i))}, device_id_type=MESH)

    scalars = [
        pltpu.make_async_copy(ref, to, l_loc.at[n])
        for n, (ref, to) in enumerate(((info_ref, info), (counts_ref, csm)))
    ]
    inputs = ((k_ref, kin), (v_ref, vin), (q_ref, qin))
    scalars[0].start()
    scalars[1].start()
    for a, (ref, to) in enumerate(inputs):
        for pair in range(HEADS // 2):
            columns = slice(2 * pair * DH, 2 * (pair + 1) * DH)
            pltpu.make_async_copy(ref.at[..., columns], to.at[pair], l_loc.at[2 + a]).start()
    def pair_of(h, p):
        return info[0, rank_at(H, pairs, h, p)]

    def row_range(owner):
        return pl.ds(pl.multiple_of(owner * rows, 16), rows)

    def piece_range(owner):
        return pl.ds(owner * (rows // piece), rows // piece)

    def staged(a, p, hs, i):
        return qs.at[p, i] if a == 2 else (ks, vs)[a].at[p, hs, i]

    def place_at(a, owner, p, hs):
        if a == 2:
            return qb[p].at[row_range(owner), :]
        return (kb, vb)[a][2 * p + hs].at[piece_range(owner)]

    def x_copy(a, p, hs, i, landed):
        at = source_of(i32(i)) if landed else me
        return pltpu.make_async_remote_copy(
            src_ref=staged(a, p, hs, i),
            dst_ref=place_at(a, at, p, hs),
            send_sem=x_send.at[a],
            recv_sem=x_recv.at[a, p, hs],
            device_id={"head": peer_of(i32(i))},
            device_id_type=MESH,
        )

    def l_copy(d):
        return pltpu.make_async_remote_copy(
            src_ref=lists_ref,
            dst_ref=lbuf.at[d - 1],
            send_sem=l_send.at[0],
            recv_sem=l_recv.at[0],
            device_id={"seq": tile_after(d)},
            device_id_type=MESH,
        )

    def z_copy(p, d, c, g, room):
        lo, hi = slot_ranges(p, c, pairs, room)[g]
        return pltpu.make_async_remote_copy(
            src_ref=pk.at[p, d - 1, c, lo:hi],
            dst_ref=fk.at[p, d - 1, c, lo:hi],
            send_sem=z_send.at[p],
            recv_sem=z_recv.at[p, c, g],
            device_id={"seq": tile_after(d)},
            device_id_type=MESH,
        )

    def o_copy(p, hs, i, landed):
        at = source_of(i) if landed else me
        return pltpu.make_async_remote_copy(
            src_ref=ob.at[p, hs, i],
            dst_ref=land.at[rank_at(H, pairs, at, p), hs],
            send_sem=o_send.at[0],
            recv_sem=o_recv.at[0],
            device_id={"head": peer_of(i)},
            device_id_type=MESH,
        )

    loaded = set()

    def x_start(a, p):
        if a not in loaded:
            loaded.add(a)
            whole = inputs[a][1]
            pltpu.make_async_copy(whole, whole, l_loc.at[2 + a]).wait()
        for hs in range(1 if a == 2 else 2):
            for i in range(H):
                pair = pair_of(peer_of(i32(i)), p)
                if a == 2:
                    taken = qin[pair]
                else:
                    taken = (kin, vin)[a][pair, :, :, hs * DH : (hs + 1) * DH]
                if i < H - 1:
                    staged(a, p, hs, i)[...] = taken
                    x_copy(a, p, hs, i, False).start()
                else:
                    place_at(a, me, p, hs)[...] = taken

    def all_of(ref, send_sem, recv_sem):
        return pltpu.make_async_remote_copy(
            src_ref=ref, dst_ref=ref, send_sem=send_sem, recv_sem=recv_sem,
            device_id={"head": peer_of(i32(0))}, device_id_type=MESH,
        )

    def x_arrived(a, p, hs):
        all_of(qs.at[p] if a == 2 else (ks, vs)[a].at[p, hs], x_send.at[a], x_recv.at[a, p, hs]).wait_recv()

    scalars[0].wait()
    pl.semaphore_wait(barrier, H - 1 + S - 1)
    for d in range(1, S):
        l_copy(d).start()
    if pairs == 4:
        order = [(0, 0), (1, 0), (0, 1), (1, 1), (2, 0), (0, 2), (0, 3), (1, 2), (2, 1), (2, 2), (1, 3), (2, 3)]
    else:
        order = [(a, p) for p in range(pairs) for a in range(3)]
    for a, p in order[:4]:
        x_start(a, p)

    scalars[1].wait()
    all_of(lbuf, l_send.at[0], l_recv.at[0]).wait_recv()
    to_scalars = pltpu.make_async_copy(lbuf, lsm, l_loc.at[5])
    to_scalars.start()
    to_scalars.wait()

    waited = set()

    def need(a, p, hs):
        if (a, p, hs) not in waited:
            waited.add((a, p, hs))
            x_arrived(a, p, hs)

    def pack(p, c, g, room):
        held = (kb, vb)[c][2 * p : 2 * p + 2]
        lo, hi = slot_ranges(p, c, pairs, room)[g]
        most = min(MOST, room)
        head = 2 * pair_of(me, p)
        for d in range(1, S):
            at = S - d - 1
            first = csm[tile_after(d), tile, head]
            for s in range(lo, hi):
                left = lsm[at, min(s, MOST - 1), tile, head]
                right = lsm[at, min(room - 1 - s, MOST - 1), tile, head + 1]
                for b in range(BLOCK // piece):
                    if s < most:
                        chosen = held[0][left * (BLOCK // piece) + b]
                    if s >= room - most:
                        other = held[1][right * (BLOCK // piece) + b]
                        chosen = jnp.where(s < first, chosen, other) if s < most else other
                    pk[p, d - 1, c, s, pl.ds(b * piece, piece), :] = chosen
            z_copy(p, d, c, g, room).start()

    def pack_place(p, c):
        if p == 0:
            need(c, p, 0)
            pack(p, c, 0, PAIR_MOST)
            need(c, p, 1)
            for g in range(1, len(slot_ranges(p, c, pairs, PAIR_MOST))):
                pack(p, c, g, PAIR_MOST)
        else:
            need(c, p, 0)
            need(c, p, 1)

            def send(room):
                for g in range(len(slot_ranges(p, c, pairs, room))):
                    pack(p, c, g, room)

            with_room(p, send)

    factor = math.log2(math.e) / math.sqrt(DH)

    def z_arrived(p, c, g, room):
        lo, hi = slot_ranges(p, c, pairs, room)[g]
        all_of(fk.at[p, :, c, lo:hi], z_send.at[p], z_recv.at[p, c, g]).wait_recv()

    def far_slots(hs, room):
        most = min(MOST, room)
        return slice(0, most) if hs == 0 else slice(room - most, room)

    def far_blocks(p, c, d, hs, room):
        return fk[p, d - 1, c, far_slots(hs, room)].reshape(min(MOST, room) * BLOCK, DH)

    def scores_of(p, hs, q, room):
        width = min(MOST, room) * BLOCK
        lane = lax.broadcasted_iota(jnp.int32, (1, width), 1)
        scores = [contract_last(q, kb[2 * p + hs][...].reshape(TILE, DH))]
        head = 2 * pair_of(me, p) + hs
        for d in range(1, S):
            used = csm[tile, lax.rem(tile + S - d, S), head] * BLOCK
            live = lane < used if hs == 0 else lane >= width - used
            bias = jnp.where(live, 0.0, -jnp.inf).astype(jnp.float32)
            scores.append(contract_last(q, far_blocks(p, 0, d, hs, room)) + bias)
        top = functools.reduce(jnp.maximum, [jnp.max(s, axis=1, keepdims=True) for s in scores])
        return scores, top

    def weigh(s, top):
        return jnp.exp2((s - top) * factor)

    def mix(w, v):
        return jnp.dot(w, v, preferred_element_type=jnp.float32)

    def finish(p, hs, i, out):
        ob[p, hs, i] = out

        @pl.when(i < H - 1)
        def _():
            o_copy(p, hs, i, False).start()

    def land_own(p, hs):
        land[rank_at(H, pairs, me, p), hs] = ob[p, hs, H - 1]

    def weigh_place(p):
        def all_chunks(room):
            width = min(MOST, room) * BLOCK
            for g in range(len(slot_ranges(p, 0, pairs, room))):
                z_arrived(p, 0, g, room)

            def chunk(i, carry):
                mine = row_range(peer_of(i))
                for hs in range(2):
                    q = qb[p][mine, hs * DH : (hs + 1) * DH]
                    scores, top = scores_of(p, hs, q, room)
                    w = weigh(scores[0], top)
                    total = jnp.sum(w, axis=1, keepdims=True)
                    mbuf[p % 2, hs, i] = mix(w.astype(jnp.bfloat16), vb[2 * p + hs][...].reshape(TILE, DH))
                    for d in range(1, S):
                        w = weigh(scores[d], top)
                        total = total + jnp.sum(w, axis=1, keepdims=True)
                        pbuf[p % 2, hs, i, :, (d - 1) * width : d * width] = w.astype(jnp.bfloat16)
                    tbuf[p % 2, hs, i] = total
                return carry

            lax.fori_loop(0, H, chunk, 0)

        need(2, p, 0)
        with_room(p, all_chunks)

    def mix_place(p):
        def all_chunks(room):
            width = min(MOST, room) * BLOCK
            groups = len(slot_ranges(p, 1, pairs, room))
            for hs in range(2):
                for g in range(groups) if p < last and hs == 0 else range(hs, hs + 1) if p == last else ():
                    z_arrived(p, 1, g, room)

                def chunk(i, carry, hs=hs):
                    mixed = mbuf[p % 2, hs, i]
                    for d in range(1, S):
                        weights = pbuf[p % 2, hs, i, :, (d - 1) * width : d * width]
                        mixed = mixed + mix(weights, far_blocks(p, 1, d, hs, room))
                    finish(p, hs, i, (mixed / tbuf[p % 2, hs, i]).astype(jnp.bfloat16))
                    return carry

                lax.fori_loop(0, H, chunk, 0)
                land_own(p, hs)

        with_room(p, all_chunks)

    pack_place(0, 0)
    pack_place(0, 1)
    for a, p in order[4:]:
        x_start(a, p)
    if pairs == 4:
        pack_place(1, 0)
        pack_place(1, 1)
        pack_place(2, 0)
        pack_place(3, 0)
        weigh_place(0)
        mix_place(0)
        pack_place(2, 1)
        weigh_place(1)
        mix_place(1)
        weigh_place(2)
        pack_place(3, 1)
        weigh_place(3)
        mix_place(2)
        mix_place(3)
    else:
        for p in range(1, pairs):
            pack_place(p, 0)
            pack_place(p, 1)
        for p in range(pairs):
            weigh_place(p)
            mix_place(p)

    sent_out = all_of(ob.at[:, :, : H - 1], o_send.at[0], o_recv.at[0])
    sent_out.wait_recv()
    for pair in range(HEADS // 2):
        rank = info[1, pair]
        for hs in range(2):
            out_ref[:, (2 * pair + hs) * DH : (2 * pair + hs + 1) * DH] = land[rank, hs]
    all_of(lbuf, l_send.at[0], l_recv.at[0]).wait_send()
    for p in range(pairs):

        def sent(room, p=p):
            all_of(pk.at[p, :, :, :room], z_send.at[p], z_recv.at[p, 0, 0]).wait_send()

        with_room(p, sent)
    for a, ref in enumerate((ks, vs, qs)):
        all_of(ref, x_send.at[a], x_recv.at[a, 0, 0]).wait_send()
    sent_out.wait_send()


def attention(dims, number, lists, counts, info, query_rows, key_rows, value_rows):
    H, S, rows, heads, piece, light = dims
    pairs = heads // 2
    bf16 = jnp.bfloat16
    chunk = (rows // piece, piece, query_rows.shape[1])
    operands = (lists, counts, info, query_rows, key_rows.reshape(chunk), value_rows.reshape(chunk))
    return pl.pallas_call(
        functools.partial(body, dims),
        out_shape=pltpu.VMEM(query_rows.shape, bf16),
        in_specs=[pl.BlockSpec(memory_space=pltpu.HBM)] * 6,
        out_specs=pl.BlockSpec(memory_space=pltpu.VMEM),
        scratch_shapes=[pltpu.VMEM((TILE // piece, piece, DH), bf16) for _ in range(4 * pairs)]
        + [pltpu.VMEM((TILE, 2 * DH), bf16) for _ in range(pairs)]
        + [
            pltpu.VMEM((HEADS // 2, rows, 2 * DH), bf16),
            pltpu.VMEM((HEADS // 2, rows // piece, piece, 2 * DH), bf16),
            pltpu.VMEM((HEADS // 2, rows // piece, piece, 2 * DH), bf16),
            pltpu.VMEM((pairs, H - 1, rows, 2 * DH), bf16),
            pltpu.VMEM((pairs, 2, H - 1, rows // piece, piece, DH), bf16),
            pltpu.VMEM((pairs, 2, H - 1, rows // piece, piece, DH), bf16),
            pltpu.VMEM((pairs, 2, H, rows, DH), bf16),
            pltpu.VMEM((HEADS // 2, 2, rows, DH), bf16),
            pltpu.VMEM((pairs, S - 1, 2, PAIR_MOST, BLOCK, DH), bf16),
            pltpu.VMEM((pairs, S - 1, 2, PAIR_MOST, BLOCK, DH), bf16),
            pltpu.VMEM((min(2, pairs), 2, H, rows, (S - 1) * MOST * BLOCK), bf16),
            pltpu.VMEM((min(2, pairs), 2, H, rows, DH), jnp.float32),
            pltpu.VMEM((min(2, pairs), 2, H, rows, 1), jnp.float32),
            pltpu.VMEM((S - 1,) + lists.shape, jnp.int32),
            pltpu.SMEM((S - 1,) + lists.shape, jnp.int32),
            pltpu.SMEM(counts.shape, jnp.int32),
            pltpu.SMEM((8, 128), jnp.int32),
            pltpu.SemaphoreType.DMA((3,)),
            pltpu.SemaphoreType.DMA((3, pairs, 2)),
            pltpu.SemaphoreType.DMA((pairs,)),
            pltpu.SemaphoreType.DMA((pairs, 2, 2)),
            pltpu.SemaphoreType.DMA((1,)),
            pltpu.SemaphoreType.DMA((1,)),
            pltpu.SemaphoreType.DMA((6,)),
            pltpu.SemaphoreType.DMA((1,)),
            pltpu.SemaphoreType.DMA((1,)),
        ],
        compiler_params=pltpu.CompilerParams(
            collective_id=number, has_side_effects=True, vmem_limit_bytes=VMEM_LIMIT
        ),
        name=f"block_attention_{light}",
    )(*operands)


def on_device(query_rows, key_rows, value_rows, block_lists, block_counts):
    H = lax.axis_size("head")
    S = lax.axis_size("seq")
    rows = query_rows.shape[0]
    heads = HEADS // H
    pairs = heads // 2
    lists = jnp.transpose(block_lists, (1, 3, 2, 0))[0]
    counts = jnp.transpose(block_counts, (1, 2, 0))
    piece = math.gcd(rows, BLOCK)
    rooms = ROOMS if pairs == 4 else (PAIR_MOST,)
    kernels = [
        functools.partial(attention, (H, S, rows, heads, piece, room), 1 + n) for n, room in enumerate(rooms)
    ]
    if len(rooms) == 1:
        info = jnp.broadcast_to(jnp.arange(128, dtype=jnp.int32), (8, 128))
        return kernels[0](lists, counts, info, query_rows, key_rows, value_rows)
    info, pick = survey(counts, lax.axis_size("parts"), H, pairs)
    return lax.switch(pick[0, 0], kernels, lists, counts, info, query_rows, key_rows, value_rows)


def solution(mesh):
    in_specs = (
        P(("parts", "seq", "head"), None),
        P(("parts", "seq", "head"), None),
        P(("parts", "seq", "head"), None),
        P("parts", "seq", None, None),
        P("parts", None, None),
    )
    out_specs = P(("parts", "seq", "head"), None)
    return jax.shard_map(
        on_device, mesh=mesh, in_specs=in_specs, out_specs=out_specs, check_vma=False
    )
```

```python
import functools
import math

import jax
import jax.numpy as jnp
from jax import lax
from jax.experimental import pallas as pl
from jax.experimental.pallas import tpu as pltpu
from jax.sharding import PartitionSpec as P

HEADS = 32
DH = 128
BLOCK = 128
MOST = 3
PAIR_MOST = 4
TILE = 768
MESH = pl.DeviceIdType.MESH
ROOMS = (1, 2, PAIR_MOST)
VMEM_LIMIT = 60 << 20


def contract_last(a, b):
    return lax.dot_general(a, b, (((1,), (1,)), ((), ())), preferred_element_type=jnp.float32)


def rank_at(H, pairs, h, p):
    if pairs != 4:
        return p * H + h
    chips = H // 2
    if p == 2:
        return 2 * H + lax.rem(h, 2) * chips + lax.div(h, 2)
    return {0: 0, 1: 3 * H, 3: H}[p] + h


def heavy_pairs(H, pairs):
    return 2 * H + H // 2 if pairs == 4 else H * pairs


def ranked(counts, H, pairs):
    total = HEADS // 2
    f32 = jnp.float32
    head_no = lax.broadcasted_iota(jnp.int32, (HEADS, total), 0)
    pair_no = lax.broadcasted_iota(jnp.int32, (HEADS, total), 1)
    in_pair = jnp.where((head_no == 2 * pair_no) | (head_no == 2 * pair_no + 1), 1.0, 0.0).astype(f32)
    most = jnp.zeros((1, total), f32)
    for t in range(counts.shape[0]):
        sums = jnp.dot(counts[t].astype(f32), in_pair, preferred_element_type=f32)
        most = jnp.maximum(most, jnp.max(sums, axis=0, keepdims=True))
    row = lax.broadcasted_iota(jnp.int32, (total, total), 0)
    col = lax.broadcasted_iota(jnp.int32, (total, total), 1)
    along = jnp.broadcast_to(most, (total, total))
    down = jnp.sum(jnp.where(row == col, along, 0.0), axis=1, keepdims=True)
    ahead = (along > down) | ((along == down) & (col < row))
    rank = jnp.sum(jnp.where(ahead, 1.0, 0.0), axis=1, keepdims=True)
    pair_at = jnp.sum(jnp.where(rank == col.astype(f32), row.astype(f32), 0.0), axis=0, keepdims=True)
    rank_of = jnp.sum(jnp.where(row == col, jnp.broadcast_to(rank, (total, total)), 0.0), axis=0, keepdims=True)
    room = jnp.sum(jnp.where(rank == float(heavy_pairs(H, pairs)), down, 0.0), axis=0, keepdims=True)
    return rank_of, pair_at, room


def survey_body(dims, counts_ref, info_ref, pick_ref, own, others, load, send, recv):
    NP, H, pairs = dims
    total = HEADS // 2
    part = lax.axis_index("parts")
    barrier = pltpu.get_barrier_semaphore()
    for d in range(1, NP):
        pl.semaphore_signal(barrier, inc=1, device_id={"parts": lax.rem(part + d, NP)}, device_id_type=MESH)
    mine = pltpu.make_async_copy(counts_ref, own, load.at[0])
    mine.start()

    def copy(d):
        return pltpu.make_async_remote_copy(
            src_ref=counts_ref,
            dst_ref=others.at[d - 1],
            send_sem=send.at[d - 1],
            recv_sem=recv.at[d - 1],
            device_id={"parts": lax.rem(part + d, NP)},
            device_id_type=MESH,
        )

    pl.semaphore_wait(barrier, NP - 1)
    for d in range(1, NP):
        copy(d).start()
    mine.wait()
    rank_of, pair_at, room = ranked(own, H, pairs)
    info_ref[0:1, :total] = pair_at.astype(jnp.int32)
    info_ref[1:2, :total] = rank_of.astype(jnp.int32)
    for d in range(1, NP):
        copy(d).wait_recv()
        room = jnp.maximum(room, ranked(others.at[d - 1], H, pairs)[2])
    pick = jnp.zeros((1, 1), jnp.int32)
    for less in ROOMS[:-1]:
        pick = pick + (room > float(less)).astype(jnp.int32)
    pick_ref[...] = pick
    for d in range(1, NP):
        copy(d).wait_send()


def survey(counts, NP, H, pairs):
    return pl.pallas_call(
        functools.partial(survey_body, (NP, H, pairs)),
        out_shape=(jax.ShapeDtypeStruct((8, 128), jnp.int32), jax.ShapeDtypeStruct((1, 1), jnp.int32)),
        in_specs=[pl.BlockSpec(memory_space=pltpu.HBM)],
        out_specs=(pl.BlockSpec(memory_space=pltpu.VMEM),) * 2,
        scratch_shapes=[
            pltpu.VMEM(counts.shape, jnp.int32),
            pltpu.VMEM((NP - 1,) + counts.shape, jnp.int32),
            pltpu.SemaphoreType.DMA((1,)),
            pltpu.SemaphoreType.DMA((NP - 1,)),
            pltpu.SemaphoreType.DMA((NP - 1,)),
        ],
        compiler_params=pltpu.CompilerParams(collective_id=0, has_side_effects=True),
        name="survey",
    )(counts)


def slot_ranges(p, c, pairs, room):
    if c == 1 and p == pairs - 1:
        return [(0, MOST), (MOST, room)]
    if p == 0:
        return [(0, 1), (1, room)]
    return [(0, room)]


def body(dims, lists_ref, counts_ref, info_ref, q_ref, k_ref, v_ref, out_ref, *scratch):
    H, S, rows, heads, piece, light = dims
    pairs = heads // 2
    last = pairs - 1
    chips = H // 2
    kb, vb, qb = scratch[: 2 * pairs], scratch[2 * pairs : 4 * pairs], scratch[4 * pairs : 5 * pairs]
    (qin, kin, vin, qs, ks, vs, ob, land, pk, fk, pbuf, mbuf, tbuf, lbuf, lsm, csm, info,
     x_send, x_recv, z_send, z_recv, l_send, l_recv, l_loc, o_send, o_recv) = scratch[5 * pairs :]
    me = lax.axis_index("head")
    tile = lax.axis_index("seq")
    core = lax.rem(me, 2)

    def peer_of(i):
        chip = lax.rem(lax.div(me, 2) + 1 + lax.div(i, 2), chips)
        return chip * 2 + lax.rem(me + i + 1, 2)

    def source_of(i):
        chip = lax.rem(lax.div(me, 2) + 2 * chips - 1 - lax.div(i, 2), chips)
        return chip * 2 + lax.rem(me + i + 1, 2)

    def tile_after(d):
        return lax.rem(tile + d, S)

    def i32(i):
        return jnp.int32(i)

    def with_room(p, what):
        if pairs != 4 or light == PAIR_MOST or p in (0, last):
            what(PAIR_MOST)
        elif p == 1:
            what(light)
        else:
            pl.when(core == 0)(lambda: what(PAIR_MOST))
            pl.when(core != 0)(lambda: what(light))

    barrier = pltpu.get_barrier_semaphore()
    for d in range(1, S):
        pl.semaphore_signal(barrier, inc=1, device_id={"seq": tile_after(d)}, device_id_type=MESH)
    for i in range(H - 1):
        pl.semaphore_signal(barrier, inc=1, device_id={"head": peer_of(i32(i))}, device_id_type=MESH)

    scalars = [
        pltpu.make_async_copy(ref, to, l_loc.at[n])
        for n, (ref, to) in enumerate(((info_ref, info), (counts_ref, csm)))
    ]
    inputs = ((k_ref, kin), (v_ref, vin), (q_ref, qin))
    scalars[0].start()
    scalars[1].start()
    for a, (ref, to) in enumerate(inputs):
        for pair in range(HEADS // 2):
            columns = slice(2 * pair * DH, 2 * (pair + 1) * DH)
            pltpu.make_async_copy(ref.at[..., columns], to.at[pair], l_loc.at[2 + a]).start()
    def pair_of(h, p):
        return info[0, rank_at(H, pairs, h, p)]

    def row_range(owner):
        return pl.ds(pl.multiple_of(owner * rows, 16), rows)

    def piece_range(owner):
        return pl.ds(owner * (rows // piece), rows // piece)

    def staged(a, p, hs, i):
        return qs.at[p, i] if a == 2 else (ks, vs)[a].at[p, hs, i]

    def place_at(a, owner, p, hs):
        if a == 2:
            return qb[p].at[row_range(owner), :]
        return (kb, vb)[a][2 * p + hs].at[piece_range(owner)]

    def x_copy(a, p, hs, i, landed):
        at = source_of(i32(i)) if landed else me
        return pltpu.make_async_remote_copy(
            src_ref=staged(a, p, hs, i),
            dst_ref=place_at(a, at, p, hs),
            send_sem=x_send.at[a],
            recv_sem=x_recv.at[a, p, hs],
            device_id={"head": peer_of(i32(i))},
            device_id_type=MESH,
        )

    def l_copy(d):
        return pltpu.make_async_remote_copy(
            src_ref=lists_ref,
            dst_ref=lsm.at[d - 1],
            send_sem=l_send.at[0],
            recv_sem=l_recv.at[0],
            device_id={"seq": tile_after(d)},
            device_id_type=MESH,
        )

    def z_copy(p, d, c, g, room):
        lo, hi = slot_ranges(p, c, pairs, room)[g]
        return pltpu.make_async_remote_copy(
            src_ref=pk.at[p, d - 1, c, lo:hi],
            dst_ref=fk.at[p, d - 1, c, lo:hi],
            send_sem=z_send.at[p],
            recv_sem=z_recv.at[p, c, g],
            device_id={"seq": tile_after(d)},
            device_id_type=MESH,
        )

    def o_copy(p, hs, i, landed):
        at = source_of(i) if landed else me
        return pltpu.make_async_remote_copy(
            src_ref=ob.at[p, hs, i],
            dst_ref=land.at[rank_at(H, pairs, at, p), hs],
            send_sem=o_send.at[0],
            recv_sem=o_recv.at[0],
            device_id={"head": peer_of(i)},
            device_id_type=MESH,
        )

    loaded = set()

    def x_start(a, p):
        if a not in loaded:
            loaded.add(a)
            whole = inputs[a][1]
            pltpu.make_async_copy(whole, whole, l_loc.at[2 + a]).wait()
        for hs in range(1 if a == 2 else 2):
            for i in range(H):
                pair = pair_of(peer_of(i32(i)), p)
                if a == 2:
                    taken = qin[pair]
                else:
                    taken = (kin, vin)[a][pair, :, :, hs * DH : (hs + 1) * DH]
                if i < H - 1:
                    staged(a, p, hs, i)[...] = taken
                    x_copy(a, p, hs, i, False).start()
                else:
                    place_at(a, me, p, hs)[...] = taken

    def all_of(ref, send_sem, recv_sem):
        return pltpu.make_async_remote_copy(
            src_ref=ref, dst_ref=ref, send_sem=send_sem, recv_sem=recv_sem,
            device_id={"head": peer_of(i32(0))}, device_id_type=MESH,
        )

    def x_arrived(a, p, hs):
        all_of(qs.at[p] if a == 2 else (ks, vs)[a].at[p, hs], x_send.at[a], x_recv.at[a, p, hs]).wait_recv()

    scalars[0].wait()
    pl.semaphore_wait(barrier, H - 1 + S - 1)
    for d in range(1, S):
        l_copy(d).start()
    if pairs == 4:
        order = [(0, 0), (1, 0), (0, 1), (1, 1), (2, 0), (0, 2), (0, 3), (1, 2), (2, 1), (2, 2), (1, 3), (2, 3)]
    else:
        order = [(a, p) for p in range(pairs) for a in range(3)]
    for a, p in order[:4]:
        x_start(a, p)

    scalars[1].wait()
    all_of(lsm, l_send.at[0], l_recv.at[0]).wait_recv()

    waited = set()

    def need(a, p, hs):
        if (a, p, hs) not in waited:
            waited.add((a, p, hs))
            x_arrived(a, p, hs)

    def pack(p, c, g, room):
        held = (kb, vb)[c][2 * p : 2 * p + 2]
        lo, hi = slot_ranges(p, c, pairs, room)[g]
        most = min(MOST, room)
        head = 2 * pair_of(me, p)
        for d in range(1, S):
            at = S - d - 1
            first = csm[tile_after(d), tile, head]
            for s in range(lo, hi):
                left = lsm[at, min(s, MOST - 1), tile, head]
                right = lsm[at, min(room - 1 - s, MOST - 1), tile, head + 1]
                for b in range(BLOCK // piece):
                    if s < most:
                        chosen = held[0][left * (BLOCK // piece) + b]
                    if s >= room - most:
                        other = held[1][right * (BLOCK // piece) + b]
                        chosen = jnp.where(s < first, chosen, other) if s < most else other
                    pk[p, d - 1, c, s, pl.ds(b * piece, piece), :] = chosen
            z_copy(p, d, c, g, room).start()

    def pack_place(p, c):
        if p == 0:
            need(c, p, 0)
            pack(p, c, 0, PAIR_MOST)
            need(c, p, 1)
            for g in range(1, len(slot_ranges(p, c, pairs, PAIR_MOST))):
                pack(p, c, g, PAIR_MOST)
        else:
            need(c, p, 0)
            need(c, p, 1)

            def send(room):
                for g in range(len(slot_ranges(p, c, pairs, room))):
                    pack(p, c, g, room)

            with_room(p, send)

    factor = math.log2(math.e) / math.sqrt(DH)

    def z_arrived(p, c, g, room):
        lo, hi = slot_ranges(p, c, pairs, room)[g]
        all_of(fk.at[p, :, c, lo:hi], z_send.at[p], z_recv.at[p, c, g]).wait_recv()

    def far_slots(hs, room):
        most = min(MOST, room)
        return slice(0, most) if hs == 0 else slice(room - most, room)

    def far_blocks(p, c, d, hs, room):
        return fk[p, d - 1, c, far_slots(hs, room)].reshape(min(MOST, room) * BLOCK, DH)

    def scores_of(p, hs, q, room):
        width = min(MOST, room) * BLOCK
        lane = lax.broadcasted_iota(jnp.int32, (1, width), 1)
        scores = [contract_last(q, kb[2 * p + hs][...].reshape(TILE, DH))]
        head = 2 * pair_of(me, p) + hs
        for d in range(1, S):
            used = csm[tile, lax.rem(tile + S - d, S), head] * BLOCK
            live = lane < used if hs == 0 else lane >= width - used
            bias = jnp.where(live, 0.0, -jnp.inf).astype(jnp.float32)
            scores.append(contract_last(q, far_blocks(p, 0, d, hs, room)) + bias)
        top = functools.reduce(jnp.maximum, [jnp.max(s, axis=1, keepdims=True) for s in scores])
        return scores, top

    def weigh(s, top):
        return jnp.exp2((s - top) * factor)

    def mix(w, v):
        return jnp.dot(w, v, preferred_element_type=jnp.float32)

    def finish(p, hs, i, out):
        ob[p, hs, i] = out

        @pl.when(i < H - 1)
        def _():
            o_copy(p, hs, i, False).start()

    def land_own(p, hs):
        land[rank_at(H, pairs, me, p), hs] = ob[p, hs, H - 1]

    def weigh_place(p):
        def all_chunks(room):
            width = min(MOST, room) * BLOCK
            for g in range(len(slot_ranges(p, 0, pairs, room))):
                z_arrived(p, 0, g, room)

            def chunk(i, carry):
                mine = row_range(peer_of(i))
                for hs in range(2):
                    q = qb[p][mine, hs * DH : (hs + 1) * DH]
                    scores, top = scores_of(p, hs, q, room)
                    w = weigh(scores[0], top)
                    total = jnp.sum(w, axis=1, keepdims=True)
                    mbuf[p % 2, hs, i] = mix(w.astype(jnp.bfloat16), vb[2 * p + hs][...].reshape(TILE, DH))
                    for d in range(1, S):
                        w = weigh(scores[d], top)
                        total = total + jnp.sum(w, axis=1, keepdims=True)
                        pbuf[p % 2, hs, i, :, (d - 1) * width : d * width] = w.astype(jnp.bfloat16)
                    tbuf[p % 2, hs, i] = total
                return carry

            lax.fori_loop(0, H, chunk, 0)

        need(2, p, 0)
        with_room(p, all_chunks)

    def mix_place(p):
        def all_chunks(room):
            width = min(MOST, room) * BLOCK
            groups = len(slot_ranges(p, 1, pairs, room))
            for hs in range(2):
                for g in range(groups) if p < last and hs == 0 else range(hs, hs + 1) if p == last else ():
                    z_arrived(p, 1, g, room)

                def chunk(i, carry, hs=hs):
                    mixed = mbuf[p % 2, hs, i]
                    for d in range(1, S):
                        weights = pbuf[p % 2, hs, i, :, (d - 1) * width : d * width]
                        mixed = mixed + mix(weights, far_blocks(p, 1, d, hs, room))
                    finish(p, hs, i, (mixed / tbuf[p % 2, hs, i]).astype(jnp.bfloat16))
                    return carry

                lax.fori_loop(0, H, chunk, 0)
                land_own(p, hs)

        with_room(p, all_chunks)

    pack_place(0, 0)
    pack_place(0, 1)
    for a, p in order[4:]:
        x_start(a, p)
    if pairs == 4:
        pack_place(1, 0)
        pack_place(1, 1)
        pack_place(2, 0)
        pack_place(3, 0)
        weigh_place(0)
        mix_place(0)
        pack_place(2, 1)
        weigh_place(1)
        mix_place(1)
        weigh_place(2)
        pack_place(3, 1)
        weigh_place(3)
        mix_place(2)
        mix_place(3)
    else:
        for p in range(1, pairs):
            pack_place(p, 0)
            pack_place(p, 1)
        for p in range(pairs):
            weigh_place(p)
            mix_place(p)

    sent_out = all_of(ob.at[:, :, : H - 1], o_send.at[0], o_recv.at[0])
    sent_out.wait_recv()
    for pair in range(HEADS // 2):
        rank = info[1, pair]
        for hs in range(2):
            out_ref[:, (2 * pair + hs) * DH : (2 * pair + hs + 1) * DH] = land[rank, hs]
    all_of(lsm, l_send.at[0], l_recv.at[0]).wait_send()
    for p in range(pairs):

        def sent(room, p=p):
            all_of(pk.at[p, :, :, :room], z_send.at[p], z_recv.at[p, 0, 0]).wait_send()

        with_room(p, sent)
    for a, ref in enumerate((ks, vs, qs)):
        all_of(ref, x_send.at[a], x_recv.at[a, 0, 0]).wait_send()
    sent_out.wait_send()


def attention(dims, number, lists, counts, info, query_rows, key_rows, value_rows):
    H, S, rows, heads, piece, light = dims
    pairs = heads // 2
    bf16 = jnp.bfloat16
    chunk = (rows // piece, piece, query_rows.shape[1])
    operands = (lists, counts, info, query_rows, key_rows.reshape(chunk), value_rows.reshape(chunk))
    return pl.pallas_call(
        functools.partial(body, dims),
        out_shape=pltpu.VMEM(query_rows.shape, bf16),
        in_specs=[pl.BlockSpec(memory_space=pltpu.HBM)] * 6,
        out_specs=pl.BlockSpec(memory_space=pltpu.VMEM),
        scratch_shapes=[pltpu.VMEM((TILE // piece, piece, DH), bf16) for _ in range(4 * pairs)]
        + [pltpu.VMEM((TILE, 2 * DH), bf16) for _ in range(pairs)]
        + [
            pltpu.VMEM((HEADS // 2, rows, 2 * DH), bf16),
            pltpu.VMEM((HEADS // 2, rows // piece, piece, 2 * DH), bf16),
            pltpu.VMEM((HEADS // 2, rows // piece, piece, 2 * DH), bf16),
            pltpu.VMEM((pairs, H - 1, rows, 2 * DH), bf16),
            pltpu.VMEM((pairs, 2, H - 1, rows // piece, piece, DH), bf16),
            pltpu.VMEM((pairs, 2, H - 1, rows // piece, piece, DH), bf16),
            pltpu.VMEM((pairs, 2, H, rows, DH), bf16),
            pltpu.VMEM((HEADS // 2, 2, rows, DH), bf16),
            pltpu.VMEM((pairs, S - 1, 2, PAIR_MOST, BLOCK, DH), bf16),
            pltpu.VMEM((pairs, S - 1, 2, PAIR_MOST, BLOCK, DH), bf16),
            pltpu.VMEM((min(2, pairs), 2, H, rows, (S - 1) * MOST * BLOCK), bf16),
            pltpu.VMEM((min(2, pairs), 2, H, rows, DH), jnp.float32),
            pltpu.VMEM((min(2, pairs), 2, H, rows, 1), jnp.float32),
            pltpu.VMEM((S - 1,) + lists.shape, jnp.int32),
            pltpu.SMEM((S - 1,) + lists.shape, jnp.int32),
            pltpu.SMEM(counts.shape, jnp.int32),
            pltpu.SMEM((8, 128), jnp.int32),
            pltpu.SemaphoreType.DMA((3,)),
            pltpu.SemaphoreType.DMA((3, pairs, 2)),
            pltpu.SemaphoreType.DMA((pairs,)),
            pltpu.SemaphoreType.DMA((pairs, 2, 2)),
            pltpu.SemaphoreType.DMA((1,)),
            pltpu.SemaphoreType.DMA((1,)),
            pltpu.SemaphoreType.DMA((6,)),
            pltpu.SemaphoreType.DMA((1,)),
            pltpu.SemaphoreType.DMA((1,)),
        ],
        compiler_params=pltpu.CompilerParams(
            collective_id=number, has_side_effects=True, vmem_limit_bytes=VMEM_LIMIT
        ),
        name=f"block_attention_{light}",
    )(*operands)


def on_device(query_rows, key_rows, value_rows, block_lists, block_counts):
    H = lax.axis_size("head")
    S = lax.axis_size("seq")
    rows = query_rows.shape[0]
    heads = HEADS // H
    pairs = heads // 2
    lists = jnp.transpose(block_lists, (1, 3, 2, 0))[0]
    counts = jnp.transpose(block_counts, (1, 2, 0))
    piece = math.gcd(rows, BLOCK)
    rooms = ROOMS if pairs == 4 else (PAIR_MOST,)
    kernels = [
        functools.partial(attention, (H, S, rows, heads, piece, room), 1 + n) for n, room in enumerate(rooms)
    ]
    if len(rooms) == 1:
        info = jnp.broadcast_to(jnp.arange(128, dtype=jnp.int32), (8, 128))
        return kernels[0](lists, counts, info, query_rows, key_rows, value_rows)
    info, pick = survey(counts, lax.axis_size("parts"), H, pairs)
    return lax.switch(pick[0, 0], kernels, lists, counts, info, query_rows, key_rows, value_rows)


def solution(mesh):
    in_specs = (
        P(("parts", "seq", "head"), None),
        P(("parts", "seq", "head"), None),
        P(("parts", "seq", "head"), None),
        P("parts", "seq", None, None),
        P("parts", None, None),
    )
    out_specs = P(("parts", "seq", "head"), None)
    return jax.shard_map(
        on_device, mesh=mesh, in_specs=in_specs, out_specs=out_specs, check_vma=False
    )
```
